32 devices in a mesh: groups: 2 (over x), adapter: 8 (over z, y), tensor: 2 (over core).
Axes of the slice: x: 2, y: 2, z: 4, core: 2. Of those that a mesh axis runs over, the one named last changes fastest.
Arguments:
- acts: bfloat16 [8, 768, 8192], P('groups', 'adapter', 'tensor'), parts along dimension 0, may hold values from -6 to 6
- value_weight: bfloat16 [8192, 1024], P('tensor'), may hold values from -0.0625 to 0.0625
- adapter_down: bfloat16 [16, 64, 8192], P('adapter', None, 'tensor'), may hold values from -0.0625 to 0.0625
- adapter_up: bfloat16 [16, 64, 1024], P('adapter', None, 'tensor'), may hold values from -0.75 to 0.75
- block_slots: int32 [8, 48], P('groups', 'adapter'), parts along dimension 0, may hold values from 0 to 2, as said below
- transfer_offset: int32 [8], P('groups'), parts along dimension 0, may hold values from 1 to 7
- transfer_slot: int32 [8, 8], P('groups', 'adapter'), parts along dimension 0, may hold values from 0 to 1
Outputs:
- mixed: bfloat16 [8, 768, 1024], P('groups', 'adapter', 'tensor'), parts along dimension 0
The draws below stay inside these ranges and needn't reach their ends.
There are 2 independent parts, one for each index of `groups`. The reference program is written for one: setup_inputs(seed, part) draws one part's arguments, and reference() takes and returns one part's arrays. A program takes and returns all parts, laid end to end along the dimension named above; an argument that names none is the same for every part. Nothing has to cross between parts.
Inputs may be any that keep to these rules, and one draw needn't show every extreme that they name: `block_slots`: slot 2 names the adapter handed over to the block's server in that step. In every step the blocks of every server use each slot below 2 at least once and slot 2 from 1 to 4 times; in every step some server uses slot 2 exactly 4 times.
All inputs are finite; a program needn't handle non-finite values.
Results may differ from the reference program's by a relative error of at most 0.0039.
Values may be sent and summed in bfloat16 or wider, within the bound.
No kernel may reach another device: no remote copies, remote signals or barrier semaphores. Data moves between devices by JAX's collectives and lax.ppermute only.
A program may use at most 64 MiB of HBM per device.

```python
import jax
import jax.numpy as jnp
from jax import lax

MODEL_WIDTH = 8192
VALUE_WIDTH = 1024
ADAPTER_RANK = 64
ADP_DEV = 2
ROWS_DEV = 96
BLOCK = 16
STEPS = 4
ROWS = 768
ADAPTER_TOTAL = 16


def draw_block_slots(key, part):
    per_device = ROWS_DEV // BLOCK
    servers = ROWS // ROWS_DEV
    most = per_device - ADP_DEV
    count_key, full_key, fill_key, order_key = jax.random.split(jax.random.fold_in(key, 17), 4)
    counts = jax.random.randint(count_key, (STEPS, servers), 1, most + 1)
    full_server = jax.random.randint(full_key, (STEPS, 1), 0, servers)
    counts = jnp.where(jnp.arange(servers)[None, :] == full_server, most, counts)
    position = jnp.arange(per_device)[None, None, :]
    fillers = jax.random.randint(fill_key, (STEPS, servers, per_device), 0, ADP_DEV)
    values = jnp.where(position < ADP_DEV, position, jnp.where(position < ADP_DEV + counts[:, :, None], ADP_DEV, fillers))
    order_keys = jax.random.split(order_key, STEPS * servers)
    orders = jax.vmap(lambda subkey: jax.random.permutation(subkey, per_device))(order_keys)
    orders = orders.reshape(STEPS, servers, per_device)
    shuffled = jnp.take_along_axis(values, orders, axis=2)
    return shuffled.reshape(STEPS, servers * per_device).astype(jnp.int32)


def plant(array, key, least, top_value):
    place = [jax.random.randint(jax.random.fold_in(key, axis), (), 0, length) for axis, length in enumerate(array.shape)]
    main_axis = array.shape.index(max(array.shape))
    neighbour = place[:main_axis] + [(place[main_axis] + 1) % array.shape[main_axis]] + place[main_axis + 1:]
    return array.at[tuple(place)].set(least).at[tuple(neighbour)].set(top_value)


def level_of(rng, extent, cuts, low, top_value):
    loudness, own = 1.0, jax.random.fold_in(rng, 6)
    for dim, parts in cuts:
        steps = jnp.exp(jax.random.uniform(jax.random.fold_in(own, dim), (parts,), jnp.float32, low / len(cuts), top_value / len(cuts)))
        loudness = loudness * jnp.repeat(steps, extent[dim] // parts).reshape([-1 if axis == dim else 1 for axis in range(len(extent))])
    return loudness


def scatter_about(rng, dims, spread, most, pieces=(), kind=jnp.bfloat16):
    array = spread * jax.random.normal(rng, dims, jnp.float32)
    if pieces:
        array = array * level_of(rng, dims, pieces, -0.22, 0.18)
    return jnp.clip(array, -most, most).astype(kind)


def setup_inputs(seed: int = 0, part: int = 0) -> dict:
    streams_of = jax.random.split(jax.random.key(seed), 8)
    part_keys = jax.random.split(jax.random.fold_in(streams_of[7], part), 8)
    return {
        "acts": scatter_about(part_keys[0], (STEPS, ROWS, MODEL_WIDTH), 1.0, 6.0, ((1, 8), (2, 2))),
        "value_weight": scatter_about(streams_of[1], (MODEL_WIDTH, VALUE_WIDTH), MODEL_WIDTH ** -0.5, 0.0625, ((0, 2),)),
        "adapter_down": scatter_about(streams_of[2], (ADAPTER_TOTAL, ADAPTER_RANK, MODEL_WIDTH), MODEL_WIDTH ** -0.5, 0.0625, ((0, 8), (2, 2))),
        "adapter_up": scatter_about(streams_of[3], (ADAPTER_TOTAL, ADAPTER_RANK, VALUE_WIDTH), ADAPTER_RANK ** -0.5, 0.75, ((0, 8), (2, 2))),
        "block_slots": draw_block_slots(jax.random.fold_in(jax.random.fold_in(streams_of[7], part), 71), part),
        "transfer_offset": plant(jax.random.randint(part_keys[5], (STEPS,), 1, ROWS // ROWS_DEV), jax.random.fold_in(part_keys[5], 1), 1, (ROWS // ROWS_DEV) - 1).astype(jnp.int32),
        "transfer_slot": plant(jax.random.randint(part_keys[6], (STEPS, ROWS // ROWS_DEV), 0, ADP_DEV), jax.random.fold_in(part_keys[6], 1), 0, ADP_DEV - 1).astype(jnp.int32),
    }


def reference(acts, value_weight, adapter_down, adapter_up, block_slots, transfer_offset, transfer_slot):
    servers = ROWS // ROWS_DEV
    per_device = ROWS_DEV // BLOCK
    block_count = ROWS // BLOCK
    owner_dev = (jnp.arange(block_count, dtype=jnp.int32) // per_device).astype(jnp.int32)
    results = []
    for step_index in range(STEPS):
        slot_ids = block_slots[step_index]
        source = ((owner_dev - transfer_offset[step_index]) % servers).astype(jnp.int32)
        handed = (source * ADP_DEV + transfer_slot[step_index][source]).astype(jnp.int32)
        adapter = jnp.where(slot_ids < ADP_DEV, owner_dev * ADP_DEV + slot_ids, handed).astype(jnp.int32)
        tokens = acts[step_index]
        base_part = jnp.dot(tokens, value_weight, preferred_element_type=jnp.float32)
        blocked = tokens.reshape(block_count, BLOCK, MODEL_WIDTH)

        def per_block(block_item):
            block_rows, adapter_number = block_item
            down_weight = adapter_down[adapter_number]
            up_weight = adapter_up[adapter_number]
            reduced = jnp.dot(block_rows, down_weight.T, preferred_element_type=jnp.float32).astype(jnp.bfloat16)
            return jnp.dot(reduced, up_weight, preferred_element_type=jnp.float32)

        low_rank = lax.map(per_block, (blocked, adapter)).reshape(ROWS, VALUE_WIDTH)
        results.append((base_part + low_rank).astype(jnp.bfloat16))
    return jnp.stack(results)
```

```python
import functools

import jax
import jax.numpy as jnp
from jax import lax
from jax.experimental import pallas as pl
from jax.experimental.pallas import tpu as pltpu
from jax.sharding import PartitionSpec as P

STRIPES = 8


def contract_last(left, right):
    return lax.dot_general(
        left, right, (((left.ndim - 1,), (right.ndim - 1,)), ((), ())), preferred_element_type=jnp.float32
    )


def cut_kernel(wide, narrow, rows, piece_ref, down_ref, up_ref, *rest):
    outs, sem = rest[:-1], rest[-1]
    copies = []
    for index, out_ref in enumerate(outs):
        start = pl.multiple_of(piece_ref[index] * rows, rows)
        copies.append(pltpu.make_async_copy(
            down_ref.at[:, pl.ds(start, rows), :], out_ref.at[:, :, pl.ds(0, wide)], sem.at[2 * index]))
        copies.append(pltpu.make_async_copy(
            up_ref.at[:, pl.ds(start, rows), :], out_ref.at[:, :, pl.ds(wide, narrow)], sem.at[2 * index + 1]))
    for copy in copies:
        copy.start()
    for copy in copies:
        copy.wait()


def cut_stripes(pieces, adapter_down, adapter_up, stripe_count):
    held, rank, wide = adapter_down.shape
    narrow = adapter_up.shape[2]
    rows = rank // STRIPES
    out = jax.ShapeDtypeStruct((held, rows, wide + narrow), adapter_down.dtype)
    return pl.pallas_call(
        functools.partial(cut_kernel, wide, narrow, rows),
        out_shape=[out] * stripe_count,
        in_specs=[pl.BlockSpec(memory_space=pltpu.SMEM)] + [pl.BlockSpec(memory_space=pl.ANY)] * 2,
        out_specs=[pl.BlockSpec(memory_space=pl.ANY)] * stripe_count,
        scratch_shapes=[pltpu.SemaphoreType.DMA((2 * stripe_count,))],
    )(pieces, adapter_down, adapter_up)


def pick_kernel(server_count, steps, held, choice_ref, *rest):
    servers, rest = rest[:server_count], rest[server_count:]
    outs, (bank, in_sem, out_sem) = rest[:STRIPES], rest[STRIPES:]
    loads = [
        pltpu.make_async_copy(ref, bank.at[pl.ds(index * held, held)], in_sem.at[index])
        for index, ref in enumerate(servers)
    ]
    for load in loads:
        load.start()
    for load in loads:
        load.wait()
    stores = [
        pltpu.make_async_copy(
            bank.at[choice_ref[asker * steps + step]], out_ref.at[step], out_sem.at[asker * steps + step])
        for asker, out_ref in enumerate(outs)
        for step in range(steps)
    ]
    for store in stores:
        store.start()
    for store in stores:
        store.wait()


def pick_stripes(choice, servers, steps):
    held, rows, width = servers[0].shape
    out = jax.ShapeDtypeStruct((steps, rows, width), servers[0].dtype)
    bank_bytes = len(servers) * held * rows * width * 2
    return pl.pallas_call(
        functools.partial(pick_kernel, len(servers), steps, held),
        out_shape=[out] * STRIPES,
        in_specs=[pl.BlockSpec(memory_space=pltpu.SMEM)] + [pl.BlockSpec(memory_space=pl.ANY)] * len(servers),
        out_specs=[pl.BlockSpec(memory_space=pl.ANY)] * STRIPES,
        scratch_shapes=[
            pltpu.VMEM((len(servers) * held, rows, width), servers[0].dtype),
            pltpu.SemaphoreType.DMA((len(servers),)),
            pltpu.SemaphoreType.DMA((STRIPES * steps,)),
        ],
        compiler_params=pltpu.CompilerParams(vmem_limit_bytes=bank_bytes + (4 << 20)),
    )(choice, *servers)


def body(acts, value_weight, adapter_down, adapter_up, block_slots, transfer_offset, transfer_slot):
    groups, servers = lax.axis_size("groups"), lax.axis_size("adapter")
    parts = STRIPES // groups
    halves = servers // parts
    steps, rows_dev, wide = acts.shape
    held, rank, _ = adapter_down.shape
    narrow = adapter_up.shape[2]
    block_rows = rows_dev // block_slots.shape[1]
    group, server = lax.axis_index("groups"), lax.axis_index("adapter")
    side = lax.axis_index("tensor")
    part = server % parts
    half = server // parts

    pieces = (group * parts + jnp.bitwise_xor(part, jnp.arange(parts, dtype=jnp.int32))).astype(jnp.int32)
    stripes = cut_stripes(pieces, adapter_down, adapter_up, parts)
    banked = [stripes[0]]
    for k in range(1, servers):
        banked.append(lax.ppermute(
            stripes[k % parts], "adapter", [(i, i ^ k) for i in range(servers)]))

    asked = transfer_offset * held + transfer_slot[:, 0]
    asked = lax.all_gather(asked, ("groups", "adapter")).reshape(groups, servers, steps)
    offsets, slots = asked // held, asked % held
    asker = jnp.bitwise_xor(group * parts + part, jnp.arange(STRIPES, dtype=jnp.int32))
    ask_group, ask_server = asker // parts, half * parts + asker % parts
    source = (ask_server[:, None] - offsets[ask_group, ask_server]) % servers
    slot = slots[ask_group[:, None], source, jnp.arange(steps)[None, :]]
    choice = (jnp.bitwise_xor(source, server) * held + slot).astype(jnp.int32).reshape(-1)

    tokens = acts.reshape(steps * rows_dev, wide)
    partial_base = jnp.dot(tokens, value_weight, preferred_element_type=jnp.float32)
    swap = [(0, 1), (1, 0)]
    half_width = partial_base.shape[1] // 2
    mine = lax.dynamic_slice_in_dim(partial_base, side * half_width, half_width, 1)
    others = lax.dynamic_slice_in_dim(partial_base, (1 - side) * half_width, half_width, 1)
    base = mine + lax.ppermute(others, "tensor", swap)
    partial_own = contract_last(tokens, adapter_down.reshape(held * rank, wide))
    own = (partial_own + lax.ppermute(partial_own, "tensor", swap)).astype(jnp.bfloat16)
    row_slot = jnp.repeat(block_slots.reshape(-1), block_rows)
    own_slot = jnp.arange(held * rank, dtype=jnp.int32) // rank
    own = jnp.where(row_slot[:, None] == own_slot[None, :], own, jnp.zeros_like(own))
    base = base + jnp.dot(own, adapter_up.reshape(held * rank, narrow), preferred_element_type=jnp.float32)

    picked = pick_stripes(choice, banked, steps)
    given = [picked[0]]
    for k in range(1, STRIPES):
        pairs = []
        for g in range(groups):
            for i in range(servers):
                other = (g * parts + i % parts) ^ k
                pairs.append((g * servers + i, (other // parts) * servers + (i // parts) * parts + other % parts))
        given.append(lax.ppermute(picked[k], ("groups", "adapter"), pairs))
    passed = jnp.concatenate(given, axis=1)
    partial_passed = lax.dot_general(
        acts, passed[:, :, :wide], (((2,), (2,)), ((0,), (0,))), preferred_element_type=jnp.float32)
    reduced = (partial_passed + lax.ppermute(partial_passed, "tensor", swap)).astype(jnp.bfloat16)
    is_passed = row_slot.reshape(steps, rows_dev, 1) == held
    reduced = jnp.where(is_passed, reduced, jnp.zeros_like(reduced))
    low_rank = lax.dot_general(
        reduced, passed[:, :, wide:], (((2,), (1,)), ((0,), (0,))), preferred_element_type=jnp.float32)
    return (base.reshape(steps, rows_dev, narrow) + low_rank).astype(jnp.bfloat16)


def solution(mesh):
    in_specs = (
        P("groups", "adapter", "tensor"),
        P("tensor", None),
        P("adapter", None, "tensor"),
        P("adapter", None, "tensor"),
        P("groups", "adapter"),
        P("groups"),
        P("groups", "adapter"),
    )
    out_specs = P("groups", "adapter", "tensor")
    return jax.shard_map(body, mesh=mesh, in_specs=in_specs, out_specs=out_specs, check_vma=False)
```

```python
import functools

import jax
import jax.numpy as jnp
from jax import lax
from jax.experimental import pallas as pl
from jax.experimental.pallas import tpu as pltpu
from jax.sharding import PartitionSpec as P

STRIPES = 8


def contract_last(left, right):
    return lax.dot_general(
        left, right, (((left.ndim - 1,), (right.ndim - 1,)), ((), ())), preferred_element_type=jnp.float32
    )


def cut_kernel(wide, piece_ref, down_ref, up_ref, *outs):
    for index, out_ref in enumerate(outs):
        out_ref[:, :, :wide] = down_ref[:, piece_ref[index]]
        out_ref[:, :, wide:] = up_ref[:, piece_ref[index]]


def cut_stripes(pieces, adapter_down, adapter_up, stripe_count):
    held, rank, wide = adapter_down.shape
    narrow = adapter_up.shape[2]
    rows = rank // STRIPES
    out = jax.ShapeDtypeStruct((held, rows, wide + narrow), adapter_down.dtype)
    vmem = pl.BlockSpec(memory_space=pltpu.VMEM)
    return pl.pallas_call(
        functools.partial(cut_kernel, wide),
        out_shape=[out] * stripe_count,
        in_specs=[pl.BlockSpec(memory_space=pltpu.SMEM), vmem, vmem],
        out_specs=[vmem] * stripe_count,
    )(
        pieces,
        adapter_down.reshape(held, STRIPES, rows, wide),
        adapter_up.reshape(held, STRIPES, rows, narrow),
    )


def pick_kernel(server_count, steps, held, choice_ref, *rest):
    servers, outs, bank = rest[:server_count], rest[server_count:-1], rest[-1]
    for index, ref in enumerate(servers):
        bank[index * held:(index + 1) * held] = ref[...]
    for asker, out_ref in enumerate(outs):
        for step in range(steps):
            out_ref[step] = bank[choice_ref[asker * steps + step]]


def pick_stripes(choice, servers, steps):
    held, rows, width = servers[0].shape
    out = jax.ShapeDtypeStruct((steps, rows, width), servers[0].dtype)
    bank_bytes = len(servers) * held * rows * width * 2
    out_bytes = STRIPES * steps * rows * width * 2
    vmem = pl.BlockSpec(memory_space=pltpu.VMEM)
    return pl.pallas_call(
        functools.partial(pick_kernel, len(servers), steps, held),
        out_shape=[out] * STRIPES,
        in_specs=[pl.BlockSpec(memory_space=pltpu.SMEM)] + [vmem] * len(servers),
        out_specs=[vmem] * STRIPES,
        scratch_shapes=[pltpu.VMEM((len(servers) * held, rows, width), servers[0].dtype)],
        compiler_params=pltpu.CompilerParams(vmem_limit_bytes=2 * bank_bytes + out_bytes + (4 << 20)),
    )(choice, *servers)


def body(acts, value_weight, adapter_down, adapter_up, block_slots, transfer_offset, transfer_slot):
    groups, servers = lax.axis_size("groups"), lax.axis_size("adapter")
    parts = STRIPES // groups
    halves = servers // parts
    steps, rows_dev, wide = acts.shape
    held, rank, _ = adapter_down.shape
    narrow = adapter_up.shape[2]
    block_rows = rows_dev // block_slots.shape[1]
    group, server = lax.axis_index("groups"), lax.axis_index("adapter")
    side = lax.axis_index("tensor")
    part = server % parts
    half = server // parts

    pieces = (group * parts + jnp.bitwise_xor(part, jnp.arange(parts, dtype=jnp.int32))).astype(jnp.int32)
    stripes = cut_stripes(pieces, adapter_down, adapter_up, parts)
    banked = [stripes[0]]
    for k in range(1, servers):
        banked.append(lax.ppermute(
            stripes[k % parts], "adapter", [(i, i ^ k) for i in range(servers)]))

    asked = transfer_offset * held + transfer_slot[:, 0]
    asked = lax.all_gather(asked, ("groups", "adapter")).reshape(groups, servers, steps)
    offsets, slots = asked // held, asked % held
    asker = jnp.bitwise_xor(group * parts + part, jnp.arange(STRIPES, dtype=jnp.int32))
    ask_group, ask_server = asker // parts, half * parts + asker % parts
    source = (ask_server[:, None] - offsets[ask_group, ask_server]) % servers
    slot = slots[ask_group[:, None], source, jnp.arange(steps)[None, :]]
    choice = (jnp.bitwise_xor(source, server) * held + slot).astype(jnp.int32).reshape(-1)

    acts, *banked[1:6] = lax.optimization_barrier((acts, *banked[1:6]))

    tokens = acts.reshape(steps * rows_dev, wide)
    partial_base = jnp.dot(tokens, value_weight, preferred_element_type=jnp.float32)
    swap = [(0, 1), (1, 0)]
    half_width = partial_base.shape[1] // 2
    mine = lax.dynamic_slice_in_dim(partial_base, side * half_width, half_width, 1)
    others = lax.dynamic_slice_in_dim(partial_base, (1 - side) * half_width, half_width, 1)
    base = mine + lax.ppermute(others, "tensor", swap)
    partial_own = contract_last(tokens, adapter_down.reshape(held * rank, wide))
    own = (partial_own + lax.ppermute(partial_own, "tensor", swap)).astype(jnp.bfloat16)
    row_slot = jnp.repeat(block_slots.reshape(-1), block_rows)
    own_slot = jnp.arange(held * rank, dtype=jnp.int32) // rank
    own = jnp.where(row_slot[:, None] == own_slot[None, :], own, jnp.zeros_like(own))
    base = base + jnp.dot(own, adapter_up.reshape(held * rank, narrow), preferred_element_type=jnp.float32)

    base, *banked = lax.optimization_barrier((base, *banked))

    picked = pick_stripes(choice, banked, steps)
    given = [picked[0]]
    for k in range(1, STRIPES):
        pairs = []
        for g in range(groups):
            for i in range(servers):
                other = (g * parts + i % parts) ^ k
                pairs.append((g * servers + i, (other // parts) * servers + (i // parts) * parts + other % parts))
        given.append(lax.ppermute(picked[k], ("groups", "adapter"), pairs))
    passed = jnp.concatenate(given, axis=1)
    partial_passed = lax.dot_general(
        acts, passed[:, :, :wide], (((2,), (2,)), ((0,), (0,))), preferred_element_type=jnp.float32)
    reduced = (partial_passed + lax.ppermute(partial_passed, "tensor", swap)).astype(jnp.bfloat16)
    is_passed = row_slot.reshape(steps, rows_dev, 1) == held
    reduced = jnp.where(is_passed, reduced, jnp.zeros_like(reduced))
    low_rank = lax.dot_general(
        reduced, passed[:, :, wide:], (((2,), (1,)), ((0,), (0,))), preferred_element_type=jnp.float32)
    return (base.reshape(steps, rows_dev, narrow) + low_rank).astype(jnp.bfloat16)


def solution(mesh):
    in_specs = (
        P("groups", "adapter", "tensor"),
        P("tensor", None),
        P("adapter", None, "tensor"),
        P("adapter", None, "tensor"),
        P("groups", "adapter"),
        P("groups"),
        P("groups", "adapter"),
    )
    out_specs = P("groups", "adapter", "tensor")
    return jax.shard_map(body, mesh=mesh, in_specs=in_specs, out_specs=out_specs, check_vma=False)
```

```python
import functools

import jax
import jax.numpy as jnp
from jax import lax
from jax.experimental import pallas as pl
from jax.experimental.pallas import tpu as pltpu
from jax.sharding import PartitionSpec as P

STRIPES = 8


def contract_last(left, right):
    return lax.dot_general(
        left, right, (((left.ndim - 1,), (right.ndim - 1,)), ((), ())), preferred_element_type=jnp.float32
    )


def cut_kernel(wide, piece_ref, down_ref, up_ref, *outs):
    for index, out_ref in enumerate(outs):
        out_ref[:, :, :wide] = down_ref[:, piece_ref[index]]
        out_ref[:, :, wide:] = up_ref[:, piece_ref[index]]


def cut_stripes(pieces, adapter_down, adapter_up, stripe_count):
    held, rank, wide = adapter_down.shape
    narrow = adapter_up.shape[2]
    rows = rank // STRIPES
    out = jax.ShapeDtypeStruct((held, rows, wide + narrow), adapter_down.dtype)
    vmem = pl.BlockSpec(memory_space=pltpu.VMEM)
    return pl.pallas_call(
        functools.partial(cut_kernel, wide),
        out_shape=[out] * stripe_count,
        in_specs=[pl.BlockSpec(memory_space=pltpu.SMEM), vmem, vmem],
        out_specs=[vmem] * stripe_count,
    )(
        pieces,
        adapter_down.reshape(held, STRIPES, rows, wide),
        adapter_up.reshape(held, STRIPES, rows, narrow),
    )


def pick_kernel(server_count, steps, held, choice_ref, *rest):
    servers, outs, bank = rest[:server_count], rest[server_count:-1], rest[-1]
    for index, ref in enumerate(servers):
        bank[index * held:(index + 1) * held] = ref[...]
    for asker, out_ref in enumerate(outs):
        for step in range(steps):
            out_ref[step] = bank[choice_ref[asker * steps + step]]


def pick_stripes(choice, servers, steps):
    held, rows, width = servers[0].shape
    out = jax.ShapeDtypeStruct((steps, rows, width), servers[0].dtype)
    bank_bytes = len(servers) * held * rows * width * 2
    out_bytes = STRIPES * steps * rows * width * 2
    vmem = pl.BlockSpec(memory_space=pltpu.VMEM)
    return pl.pallas_call(
        functools.partial(pick_kernel, len(servers), steps, held),
        out_shape=[out] * STRIPES,
        in_specs=[pl.BlockSpec(memory_space=pltpu.SMEM)] + [vmem] * len(servers),
        out_specs=[vmem] * STRIPES,
        scratch_shapes=[pltpu.VMEM((len(servers) * held, rows, width), servers[0].dtype)],
        compiler_params=pltpu.CompilerParams(vmem_limit_bytes=2 * bank_bytes + out_bytes + (4 << 20)),
    )(choice, *servers)


def body(acts, value_weight, adapter_down, adapter_up, block_slots, transfer_offset, transfer_slot):
    groups, servers = lax.axis_size("groups"), lax.axis_size("adapter")
    parts = STRIPES // groups
    halves = servers // parts
    steps, rows_dev, wide = acts.shape
    held, rank, _ = adapter_down.shape
    narrow = adapter_up.shape[2]
    block_rows = rows_dev // block_slots.shape[1]
    group, server = lax.axis_index("groups"), lax.axis_index("adapter")
    side = lax.axis_index("tensor")
    part = server % parts
    half = server // parts

    pieces = (group * parts + jnp.bitwise_xor(part, jnp.arange(parts, dtype=jnp.int32))).astype(jnp.int32)
    stripes = cut_stripes(pieces, adapter_down, adapter_up, parts)
    banked = [stripes[0]]
    for k in range(1, servers):
        banked.append(lax.ppermute(
            stripes[k % parts], "adapter", [(i, i ^ k) for i in range(servers)]))

    transfer_slot, *banked[1:3] = lax.optimization_barrier((transfer_slot, *banked[1:3]))

    asked = transfer_offset * held + transfer_slot[:, 0]
    asked = lax.all_gather(asked, ("groups", "adapter")).reshape(groups, servers, steps)
    offsets, slots = asked // held, asked % held
    asker = jnp.bitwise_xor(group * parts + part, jnp.arange(STRIPES, dtype=jnp.int32))
    ask_group, ask_server = asker // parts, half * parts + asker % parts
    source = (ask_server[:, None] - offsets[ask_group, ask_server]) % servers
    slot = slots[ask_group[:, None], source, jnp.arange(steps)[None, :]]
    choice = (jnp.bitwise_xor(source, server) * held + slot).astype(jnp.int32).reshape(-1)

    picked = pick_stripes(choice, banked, steps)
    given = [picked[0]]
    for k in range(1, STRIPES):
        pairs = []
        for g in range(groups):
            for i in range(servers):
                other = (g * parts + i % parts) ^ k
                pairs.append((g * servers + i, (other // parts) * servers + (i // parts) * parts + other % parts))
        given.append(lax.ppermute(picked[k], ("groups", "adapter"), pairs))

    acts, *given[1:4] = lax.optimization_barrier((acts, *given[1:4]))

    tokens = acts.reshape(steps * rows_dev, wide)
    partial_base = jnp.dot(tokens, value_weight, preferred_element_type=jnp.float32)
    swap = [(0, 1), (1, 0)]
    half_width = partial_base.shape[1] // 2
    mine = lax.dynamic_slice_in_dim(partial_base, side * half_width, half_width, 1)
    others = lax.dynamic_slice_in_dim(partial_base, (1 - side) * half_width, half_width, 1)
    base = mine + lax.ppermute(others, "tensor", swap)
    partial_own = contract_last(tokens, adapter_down.reshape(held * rank, wide))
    own = (partial_own + lax.ppermute(partial_own, "tensor", swap)).astype(jnp.bfloat16)
    row_slot = jnp.repeat(block_slots.reshape(-1), block_rows)
    own_slot = jnp.arange(held * rank, dtype=jnp.int32) // rank
    own = jnp.where(row_slot[:, None] == own_slot[None, :], own, jnp.zeros_like(own))
    base = base + jnp.dot(own, adapter_up.reshape(held * rank, narrow), preferred_element_type=jnp.float32)

    base, *given[4:] = lax.optimization_barrier((base, *given[4:]))

    passed = jnp.concatenate(given, axis=1)
    partial_passed = lax.dot_general(
        acts, passed[:, :, :wide], (((2,), (2,)), ((0,), (0,))), preferred_element_type=jnp.float32)
    reduced = (partial_passed + lax.ppermute(partial_passed, "tensor", swap)).astype(jnp.bfloat16)
    is_passed = row_slot.reshape(steps, rows_dev, 1) == held
    reduced = jnp.where(is_passed, reduced, jnp.zeros_like(reduced))
    low_rank = lax.dot_general(
        reduced, passed[:, :, wide:], (((2,), (1,)), ((0,), (0,))), preferred_element_type=jnp.float32)
    return (base.reshape(steps, rows_dev, narrow) + low_rank).astype(jnp.bfloat16)


def solution(mesh):
    in_specs = (
        P("groups", "adapter", "tensor"),
        P("tensor", None),
        P("adapter", None, "tensor"),
        P("adapter", None, "tensor"),
        P("groups", "adapter"),
        P("groups"),
        P("groups", "adapter"),
    )
    out_specs = P("groups", "adapter", "tensor")
    return jax.shard_map(body, mesh=mesh, in_specs=in_specs, out_specs=out_specs, check_vma=False)
```

```python
import functools

import jax
import jax.numpy as jnp
from jax import lax
from jax.experimental import pallas as pl
from jax.experimental.pallas import tpu as pltpu
from jax.sharding import PartitionSpec as P

STRIPES = 8


def contract_last(left, right):
    return lax.dot_general(
        left, right, (((left.ndim - 1,), (right.ndim - 1,)), ((), ())), preferred_element_type=jnp.float32
    )


def cut_kernel(wide, piece_ref, down_ref, up_ref, *outs):
    for index, out_ref in enumerate(outs):
        out_ref[:, :, :wide] = down_ref[:, piece_ref[index]]
        out_ref[:, :, wide:] = up_ref[:, piece_ref[index]]


def cut_stripes(pieces, adapter_down, adapter_up, stripe_count):
    held, rank, wide = adapter_down.shape
    narrow = adapter_up.shape[2]
    rows = rank // STRIPES
    out = jax.ShapeDtypeStruct((held, rows, wide + narrow), adapter_down.dtype)
    vmem = pl.BlockSpec(memory_space=pltpu.VMEM)
    return pl.pallas_call(
        functools.partial(cut_kernel, wide),
        out_shape=[out] * stripe_count,
        in_specs=[pl.BlockSpec(memory_space=pltpu.SMEM), vmem, vmem],
        out_specs=[vmem] * stripe_count,
    )(
        pieces,
        adapter_down.reshape(held, STRIPES, rows, wide),
        adapter_up.reshape(held, STRIPES, rows, narrow),
    )


def pick_kernel(server_count, steps, held, choice_ref, *rest):
    servers, outs, bank = rest[:server_count], rest[server_count:-1], rest[-1]
    for index, ref in enumerate(servers):
        bank[index * held:(index + 1) * held] = ref[...]
    for asker, out_ref in enumerate(outs):
        for step in range(steps):
            out_ref[step] = bank[choice_ref[asker * steps + step]]


def pick_stripes(choice, servers, steps):
    held, rows, width = servers[0].shape
    out = jax.ShapeDtypeStruct((steps, rows, width), servers[0].dtype)
    bank_bytes = len(servers) * held * rows * width * 2
    out_bytes = STRIPES * steps * rows * width * 2
    vmem = pl.BlockSpec(memory_space=pltpu.VMEM)
    return pl.pallas_call(
        functools.partial(pick_kernel, len(servers), steps, held),
        out_shape=[out] * STRIPES,
        in_specs=[pl.BlockSpec(memory_space=pltpu.SMEM)] + [vmem] * len(servers),
        out_specs=[vmem] * STRIPES,
        scratch_shapes=[pltpu.VMEM((len(servers) * held, rows, width), servers[0].dtype)],
        compiler_params=pltpu.CompilerParams(vmem_limit_bytes=2 * bank_bytes + out_bytes + (4 << 20)),
    )(choice, *servers)


def products_kernel(side_ref, acts_ref, weight_ref, down_ref, send_ref, keep_ref):
    step = pl.program_id(0)
    blocks, width = pl.num_programs(0) // 2, weight_ref.shape[1]
    narrow = send_ref.shape[1] - down_ref.shape[0]
    product = jnp.dot(acts_ref[...], weight_ref[...], preferred_element_type=jnp.float32)
    for block in range(narrow // width):
        @pl.when(step == block)
        def _():
            send_ref[:, block * width:(block + 1) * width] = product

        @pl.when(step == blocks + block)
        def _():
            keep_ref[:, block * width:(block + 1) * width] = product

    @pl.when(step == 0)
    def _():
        own = contract_last(acts_ref[...], down_ref[...])
        send_ref[:, narrow:] = own
        keep_ref[:, narrow:] = own


def products(side, tokens, weight, down):
    rows, depth = tokens.shape
    columns = weight.shape[1]
    width = 256
    blocks = columns // 2 // width
    out = jax.ShapeDtypeStruct((rows, columns // 2 + down.shape[0]), jnp.float32)

    def weight_block(step, side_ref):
        half = jnp.where(step < blocks, 1 - side_ref[0], side_ref[0])
        return 0, half * blocks + step % blocks

    def whole(step, side_ref):
        return 0, 0

    return pl.pallas_call(
        products_kernel,
        out_shape=[out, out],
        grid_spec=pltpu.PrefetchScalarGridSpec(
            num_scalar_prefetch=1,
            grid=(2 * blocks,),
            in_specs=[
                pl.BlockSpec(tokens.shape, whole),
                pl.BlockSpec((depth, width), weight_block),
                pl.BlockSpec(down.shape, whole),
            ],
            out_specs=[pl.BlockSpec(out.shape, whole)] * 2,
        ),
        compiler_params=pltpu.CompilerParams(vmem_limit_bytes=48 << 20),
        cost_estimate=pl.CostEstimate(flops=0, bytes_accessed=0, transcendentals=0),
    )(side, tokens, weight, down)


def final_kernel(slots_ref, keep_ref, arrived_ref, partial_ref, other_ref, own_up_ref, up_ref, out_ref, own, passed):
    steps, rows, narrow = out_ref.shape
    rank, held = up_ref.shape[1], own_up_ref.shape[0] // up_ref.shape[1]
    block_rows = rows // slots_ref.shape[1]
    for step in range(steps):
        for block in range(slots_ref.shape[1]):
            slot = slots_ref[step, block]
            here = slice(step * rows + block * block_rows, step * rows + (block + 1) * block_rows)
            mine = (keep_ref[here, narrow:] + arrived_ref[here, narrow:]).astype(own.dtype)
            column = lax.broadcasted_iota(jnp.int32, mine.shape, 1) // rank
            own[here] = jnp.where(column == slot, mine, jnp.zeros_like(mine))
            given = (partial_ref[here] + other_ref[here]).astype(passed.dtype)
            passed[here] = jnp.where(slot == held, given, jnp.zeros_like(given))
    for step in range(steps):
        here = slice(step * rows, (step + 1) * rows)
        base = keep_ref[here, :narrow] + arrived_ref[here, :narrow]
        base += jnp.dot(own[here], own_up_ref[...], preferred_element_type=jnp.float32)
        base += jnp.dot(passed[here], up_ref[step], preferred_element_type=jnp.float32)
        out_ref[step] = base.astype(out_ref.dtype)


def finish(slots, keep, arrived, partial, other, own_up, handed):
    steps, rank, both = handed.shape
    held_rank, narrow = own_up.shape
    rows = keep.shape[0]
    vmem = pl.BlockSpec(memory_space=pltpu.VMEM)
    last = both // narrow - 1
    return pl.pallas_call(
        final_kernel,
        out_shape=jax.ShapeDtypeStruct((steps, rows // steps, narrow), jnp.bfloat16),
        grid=(1,),
        in_specs=[pl.BlockSpec(memory_space=pltpu.SMEM)] + [vmem] * 5
        + [pl.BlockSpec((steps, rank, narrow), lambda step: (0, 0, last))],
        out_specs=vmem,
        scratch_shapes=[
            pltpu.VMEM((rows, held_rank), jnp.bfloat16),
            pltpu.VMEM((rows, rank), jnp.bfloat16),
        ],
    )(slots, keep, arrived, partial, other, own_up, handed)


def rank_kernel(acts_ref, handed_ref, out_ref):
    steps, rows, wide = acts_ref.shape
    for step in range(steps):
        out_ref[step * rows:(step + 1) * rows] = contract_last(acts_ref[step], handed_ref[step, :, :wide])


def rank_part(acts, handed):
    steps, rows, _ = acts.shape
    vmem = pl.BlockSpec(memory_space=pltpu.VMEM)
    return pl.pallas_call(
        rank_kernel,
        out_shape=jax.ShapeDtypeStruct((steps * rows, handed.shape[1]), jnp.float32),
        in_specs=[vmem, vmem],
        out_specs=vmem,
        compiler_params=pltpu.CompilerParams(vmem_limit_bytes=16 << 20),
    )(acts, handed)


def body(acts, value_weight, adapter_down, adapter_up, block_slots, transfer_offset, transfer_slot):
    groups, servers = lax.axis_size("groups"), lax.axis_size("adapter")
    parts = STRIPES // groups
    halves = servers // parts
    steps, rows_dev, wide = acts.shape
    held, rank, _ = adapter_down.shape
    narrow = adapter_up.shape[2]
    group, server = lax.axis_index("groups"), lax.axis_index("adapter")
    side = lax.axis_index("tensor")
    part = server % parts
    half = server // parts

    pieces = (group * parts + jnp.bitwise_xor(part, jnp.arange(parts, dtype=jnp.int32))).astype(jnp.int32)
    stripes = cut_stripes(pieces, adapter_down, adapter_up, parts)
    banked = {0: stripes[0]}
    for k in [1, 2, 3, 4, 5, 6, 7, *range(STRIPES, servers)]:
        banked[k] = lax.ppermute(stripes[k % parts], "adapter", [(i, i ^ k) for i in range(servers)])
    early = [1, 2]
    transfer_slot, *arrived = lax.optimization_barrier((transfer_slot, *[banked[k] for k in early]))
    banked.update(zip(early, arrived))
    banked = [banked[k] for k in range(servers)]

    asked = transfer_offset * held + transfer_slot[:, 0]
    asked = lax.all_gather(asked, ("groups", "adapter")).reshape(groups, servers, steps)
    offsets, slots = asked // held, asked % held
    asker = jnp.bitwise_xor(group * parts + part, jnp.arange(STRIPES, dtype=jnp.int32))
    ask_group, ask_server = asker // parts, half * parts + asker % parts
    source = (ask_server[:, None] - offsets[ask_group, ask_server]) % servers
    slot = slots[ask_group[:, None], source, jnp.arange(steps)[None, :]]
    choice = (jnp.bitwise_xor(source, server) * held + slot).astype(jnp.int32).reshape(-1)

    picked = pick_stripes(choice, banked, steps)
    given = {0: picked[0]}
    for k in (4, 1, 2, 7, 3, 5, 6):
        pairs = []
        for g in range(groups):
            for i in range(servers):
                other = (g * parts + i % parts) ^ k
                pairs.append((g * servers + i, (other // parts) * servers + (i // parts) * parts + other % parts))
        given[k] = lax.ppermute(picked[k], ("groups", "adapter"), pairs)
    early = [4, 1, 2]
    acts, *arrived = lax.optimization_barrier((acts, *[given[k] for k in early]))
    given.update(zip(early, arrived))
    late = [k for k in range(1, STRIPES) if k not in early]

    swap = [(0, 1), (1, 0)]
    send, keep = products(
        side.astype(jnp.int32)[None], acts.reshape(steps * rows_dev, wide), value_weight,
        adapter_down.reshape(held * rank, wide))
    arrived = lax.ppermute(send, "tensor", swap)
    arrived, *others = lax.optimization_barrier((arrived, *[given[k] for k in late]))
    given.update(zip(late, others))

    handed = jnp.concatenate([given[k] for k in range(STRIPES)], axis=1)
    partial = rank_part(acts, handed)
    other = lax.ppermute(partial, "tensor", swap)
    return finish(
        block_slots, keep, arrived, partial, other, adapter_up.reshape(held * rank, narrow), handed)


def solution(mesh):
    in_specs = (
        P("groups", "adapter", "tensor"),
        P("tensor", None),
        P("adapter", None, "tensor"),
        P("adapter", None, "tensor"),
        P("groups", "adapter"),
        P("groups"),
        P("groups", "adapter"),
    )
    out_specs = P("groups", "adapter", "tensor")
    return jax.shard_map(body, mesh=mesh, in_specs=in_specs, out_specs=out_specs, check_vma=False)
```

```python
import functools

import jax
import jax.numpy as jnp
from jax import lax
from jax.experimental import pallas as pl
from jax.experimental.pallas import tpu as pltpu
from jax.sharding import PartitionSpec as P

STRIPES = 8


def contract_last(left, right):
    return lax.dot_general(
        left, right, (((left.ndim - 1,), (right.ndim - 1,)), ((), ())), preferred_element_type=jnp.float32
    )


def place():
    parts = STRIPES // lax.axis_size("groups")
    group, server = lax.axis_index("groups"), lax.axis_index("adapter")
    return group, server, lax.rem(server, parts), lax.div(server, parts)


def cut_kernel(down_ref, up_ref, *outs):
    wide = down_ref.shape[-1]
    group, _, part, _ = place()
    for index, out_ref in enumerate(outs):
        stripe = group * len(outs) + jnp.bitwise_xor(part, index)
        out_ref[:, :, :wide] = down_ref[:, stripe]
        out_ref[:, :, wide:] = up_ref[:, stripe]


def cut_stripes(adapter_down, adapter_up, stripe_count):
    held, rank, wide = adapter_down.shape
    narrow = adapter_up.shape[2]
    rows = rank // STRIPES
    out = jax.ShapeDtypeStruct((held, rows, wide + narrow), adapter_down.dtype)
    vmem = pl.BlockSpec(memory_space=pltpu.VMEM)
    return pl.pallas_call(
        cut_kernel,
        out_shape=[out] * stripe_count,
        in_specs=[vmem, vmem],
        out_specs=[vmem] * stripe_count,
        compiler_params=pltpu.CompilerParams(vmem_limit_bytes=8 << 20),
    )(
        adapter_down.reshape(held, STRIPES, rows, wide),
        adapter_up.reshape(held, STRIPES, rows, narrow),
    )


def pick_kernel(server_count, steps, held, asked_ref, *rest):
    servers, outs, bank = rest[:server_count], rest[server_count:-1], rest[-1]
    for index, ref in enumerate(servers):
        bank[index * held:(index + 1) * held] = ref[...]
    parts = STRIPES // lax.axis_size("groups")
    group, server, part, half = place()
    for index, out_ref in enumerate(outs):
        asker_group = jnp.bitwise_xor(group, index // parts)
        asker = half * parts + jnp.bitwise_xor(part, index % parts)
        for step in range(steps):
            table = asker_group * server_count
            offset = lax.div(asked_ref[(table + asker) * steps + step], held)
            source = lax.rem(asker - offset + server_count, server_count)
            slot = lax.rem(asked_ref[(table + source) * steps + step], held)
            out_ref[step] = bank[jnp.bitwise_xor(source, server) * held + slot]


def pick_stripes(asked, servers, steps):
    held, rows, width = servers[0].shape
    out = jax.ShapeDtypeStruct((steps, rows, width), servers[0].dtype)
    bank_bytes = len(servers) * held * rows * width * 2
    out_bytes = STRIPES * steps * rows * width * 2
    vmem = pl.BlockSpec(memory_space=pltpu.VMEM)
    return pl.pallas_call(
        functools.partial(pick_kernel, len(servers), steps, held),
        out_shape=[out] * STRIPES,
        in_specs=[pl.BlockSpec(memory_space=pltpu.SMEM)] + [vmem] * len(servers),
        out_specs=[vmem] * STRIPES,
        scratch_shapes=[pltpu.VMEM((len(servers) * held, rows, width), servers[0].dtype)],
        compiler_params=pltpu.CompilerParams(vmem_limit_bytes=2 * bank_bytes + out_bytes + (4 << 20)),
    )(asked, *servers)


def products_kernel(side_ref, acts_ref, weight_ref, down_ref, send_ref, keep_ref):
    step = pl.program_id(0)
    blocks, width = pl.num_programs(0) // 2, weight_ref.shape[1]
    narrow = send_ref.shape[1] - down_ref.shape[0]
    product = jnp.dot(acts_ref[...], weight_ref[...], preferred_element_type=jnp.float32)
    for block in range(narrow // width):
        @pl.when(step == block)
        def _():
            send_ref[:, block * width:(block + 1) * width] = product

        @pl.when(step == blocks + block)
        def _():
            keep_ref[:, block * width:(block + 1) * width] = product

    @pl.when(step == 0)
    def _():
        own = contract_last(acts_ref[...], down_ref[...])
        send_ref[:, narrow:] = own
        keep_ref[:, narrow:] = own


def products(side, tokens, weight, down):
    rows, depth = tokens.shape
    columns = weight.shape[1]
    width = 256
    blocks = columns // 2 // width
    out = jax.ShapeDtypeStruct((rows, columns // 2 + down.shape[0]), jnp.float32)

    def weight_block(step, side_ref):
        half = jnp.where(step < blocks, 1 - side_ref[0], side_ref[0])
        return 0, half * blocks + step % blocks

    def whole(step, side_ref):
        return 0, 0

    return pl.pallas_call(
        products_kernel,
        out_shape=[out, out],
        grid_spec=pltpu.PrefetchScalarGridSpec(
            num_scalar_prefetch=1,
            grid=(2 * blocks,),
            in_specs=[
                pl.BlockSpec(tokens.shape, whole),
                pl.BlockSpec((depth, width), weight_block),
                pl.BlockSpec(down.shape, whole),
            ],
            out_specs=[pl.BlockSpec(out.shape, whole)] * 2,
        ),
        compiler_params=pltpu.CompilerParams(vmem_limit_bytes=48 << 20),
        cost_estimate=pl.CostEstimate(flops=0, bytes_accessed=0, transcendentals=0),
    )(side, tokens, weight, down)


def final_kernel(slots_ref, keep_ref, arrived_ref, partial_ref, other_ref, own_up_ref, up_ref, out_ref, own, passed):
    steps, rows, narrow = out_ref.shape
    _, rank, both = up_ref.shape
    held = own_up_ref.shape[0] // rank
    block_rows = rows // slots_ref.shape[1]
    for step in range(steps):
        for block in range(slots_ref.shape[1]):
            slot = slots_ref[step, block]
            here = slice(step * rows + block * block_rows, step * rows + (block + 1) * block_rows)
            mine = (keep_ref[here, narrow:] + arrived_ref[here, narrow:]).astype(own.dtype)
            column = lax.broadcasted_iota(jnp.int32, mine.shape, 1) // rank
            own[here] = jnp.where(column == slot, mine, jnp.zeros_like(mine))
            given = (partial_ref[here] + other_ref[here]).astype(passed.dtype)
            passed[here] = jnp.where(slot == held, given, jnp.zeros_like(given))
    for step in range(steps):
        here = slice(step * rows, (step + 1) * rows)
        base = keep_ref[here, :narrow] + arrived_ref[here, :narrow]
        base += jnp.dot(own[here], own_up_ref[...], preferred_element_type=jnp.float32)
        base += jnp.dot(passed[here], up_ref[step, :, both - narrow:], preferred_element_type=jnp.float32)
        out_ref[step] = base.astype(out_ref.dtype)


def finish(slots, keep, arrived, partial, other, own_up, handed):
    steps, rank, _ = handed.shape
    held_rank, narrow = own_up.shape
    rows = keep.shape[0]
    vmem = pl.BlockSpec(memory_space=pltpu.VMEM)
    return pl.pallas_call(
        final_kernel,
        out_shape=jax.ShapeDtypeStruct((steps, rows // steps, narrow), jnp.bfloat16),
        in_specs=[pl.BlockSpec(memory_space=pltpu.SMEM)] + [vmem] * 6,
        out_specs=vmem,
        scratch_shapes=[
            pltpu.VMEM((rows, held_rank), jnp.bfloat16),
            pltpu.VMEM((rows, rank), jnp.bfloat16),
        ],
        compiler_params=pltpu.CompilerParams(vmem_limit_bytes=12 << 20),
    )(slots, keep, arrived, partial, other, own_up, handed)


def rank_kernel(acts_ref, handed_ref, out_ref):
    steps, rows, wide = acts_ref.shape
    for step in range(steps):
        out_ref[step * rows:(step + 1) * rows] = contract_last(acts_ref[step], handed_ref[step, :, :wide])


def rank_part(acts, handed):
    steps, rows, _ = acts.shape
    vmem = pl.BlockSpec(memory_space=pltpu.VMEM)
    return pl.pallas_call(
        rank_kernel,
        out_shape=jax.ShapeDtypeStruct((steps * rows, handed.shape[1]), jnp.float32),
        in_specs=[vmem, vmem],
        out_specs=vmem,
        compiler_params=pltpu.CompilerParams(vmem_limit_bytes=16 << 20),
    )(acts, handed)


def body(acts, value_weight, adapter_down, adapter_up, block_slots, transfer_offset, transfer_slot):
    groups, servers = lax.axis_size("groups"), lax.axis_size("adapter")
    parts = STRIPES // groups
    steps, rows_dev, wide = acts.shape
    held, rank, _ = adapter_down.shape
    narrow = adapter_up.shape[2]
    side = lax.axis_index("tensor")

    stripes = cut_stripes(adapter_down, adapter_up, parts)
    banked = {0: stripes[0]}
    for k in [1, 2, 3, 4, 5, 6, 7, *range(STRIPES, servers)]:
        banked[k] = lax.ppermute(stripes[k % parts], "adapter", [(i, i ^ k) for i in range(servers)])
    early = [1, 2]
    transfer_slot, *arrived = lax.optimization_barrier((transfer_slot, *[banked[k] for k in early]))
    banked.update(zip(early, arrived))
    banked = [banked[k] for k in range(servers)]

    asked = transfer_offset * held + transfer_slot[:, 0]
    asked = lax.all_gather(asked, ("groups", "adapter")).reshape(-1)

    picked = pick_stripes(asked, banked, steps)
    given = {0: picked[0]}
    for k in (4, 1, 2, 7, 3, 5, 6):
        pairs = []
        for g in range(groups):
            for i in range(servers):
                other = (g * parts + i % parts) ^ k
                pairs.append((g * servers + i, (other // parts) * servers + (i // parts) * parts + other % parts))
        given[k] = lax.ppermute(picked[k], ("groups", "adapter"), pairs)
    early = [4, 1, 2]
    acts, *arrived = lax.optimization_barrier((acts, *[given[k] for k in early]))
    given.update(zip(early, arrived))
    late = [k for k in range(1, STRIPES) if k not in early]

    swap = [(0, 1), (1, 0)]
    send, keep = products(
        side.astype(jnp.int32)[None], acts.reshape(steps * rows_dev, wide), value_weight,
        adapter_down.reshape(held * rank, wide))
    arrived = lax.ppermute(send, "tensor", swap)
    arrived, *others = lax.optimization_barrier((arrived, *[given[k] for k in late]))
    given.update(zip(late, others))

    handed = jnp.concatenate([given[k] for k in range(STRIPES)], axis=1)
    partial = rank_part(acts, handed)
    other = lax.ppermute(partial, "tensor", swap)
    return finish(
        block_slots, keep, arrived, partial, other, adapter_up.reshape(held * rank, narrow), handed)


def solution(mesh):
    in_specs = (
        P("groups", "adapter", "tensor"),
        P("tensor", None),
        P("adapter", None, "tensor"),
        P("adapter", None, "tensor"),
        P("groups", "adapter"),
        P("groups"),
        P("groups", "adapter"),
    )
    out_specs = P("groups", "adapter", "tensor")
    return jax.shard_map(body, mesh=mesh, in_specs=in_specs, out_specs=out_specs, check_vma=False)
```

```python
import functools

import jax
import jax.numpy as jnp
from jax import lax
from jax.experimental import pallas as pl
from jax.experimental.pallas import tpu as pltpu
from jax.sharding import PartitionSpec as P

STRIPES = 8


def contract_last(left, right):
    return lax.dot_general(
        left, right, (((left.ndim - 1,), (right.ndim - 1,)), ((), ())), preferred_element_type=jnp.float32
    )


def place():
    parts = STRIPES // lax.axis_size("groups")
    group, server = lax.axis_index("groups"), lax.axis_index("adapter")
    return group, server, lax.rem(server, parts), lax.div(server, parts)


def cut_kernel(down_ref, up_ref, *outs):
    wide = down_ref.shape[-1]
    group, _, part, _ = place()
    for index, out_ref in enumerate(outs):
        stripe = group * len(outs) + jnp.bitwise_xor(part, index)
        out_ref[:, :, :wide] = down_ref[:, stripe]
        out_ref[:, :, wide:] = up_ref[:, stripe]


def cut_stripes(adapter_down, adapter_up, stripe_count):
    held, rank, wide = adapter_down.shape
    narrow = adapter_up.shape[2]
    rows = rank // STRIPES
    out = jax.ShapeDtypeStruct((held, rows, wide + narrow), adapter_down.dtype)
    vmem = pl.BlockSpec(memory_space=pltpu.VMEM)
    return pl.pallas_call(
        cut_kernel,
        out_shape=[out] * stripe_count,
        in_specs=[vmem, vmem],
        out_specs=[vmem] * stripe_count,
        compiler_params=pltpu.CompilerParams(vmem_limit_bytes=8 << 20),
    )(
        adapter_down.reshape(held, STRIPES, rows, wide),
        adapter_up.reshape(held, STRIPES, rows, narrow),
    )


def pick_kernel(server_count, steps, held, asked_ref, *rest):
    servers, outs, bank = rest[:server_count], rest[server_count:-1], rest[-1]
    for index, ref in enumerate(servers):
        bank[index * held:(index + 1) * held] = ref[...]
    parts = STRIPES // lax.axis_size("groups")
    group, server, part, half = place()
    for index, out_ref in enumerate(outs):
        asker_group = jnp.bitwise_xor(group, index // parts)
        asker = half * parts + jnp.bitwise_xor(part, index % parts)
        for step in range(steps):
            table = asker_group * server_count
            offset = lax.div(asked_ref[(table + asker) * steps + step], held)
            source = lax.rem(asker - offset + server_count, server_count)
            slot = lax.rem(asked_ref[(table + source) * steps + step], held)
            out_ref[step] = bank[jnp.bitwise_xor(source, server) * held + slot]


def pick_stripes(asked, servers, steps):
    held, rows, width = servers[0].shape
    out = jax.ShapeDtypeStruct((steps, rows, width), servers[0].dtype)
    bank_bytes = len(servers) * held * rows * width * 2
    out_bytes = STRIPES * steps * rows * width * 2
    vmem = pl.BlockSpec(memory_space=pltpu.VMEM)
    return pl.pallas_call(
        functools.partial(pick_kernel, len(servers), steps, held),
        out_shape=[out] * STRIPES,
        in_specs=[pl.BlockSpec(memory_space=pltpu.SMEM)] + [vmem] * len(servers),
        out_specs=[vmem] * STRIPES,
        scratch_shapes=[pltpu.VMEM((len(servers) * held, rows, width), servers[0].dtype)],
        compiler_params=pltpu.CompilerParams(vmem_limit_bytes=2 * bank_bytes + out_bytes + (4 << 20)),
    )(asked, *servers)


def product_kernel(half_ref, acts_ref, weight_ref, *rest):
    out_ref = rest[-1]
    step = pl.program_id(0)
    width = weight_ref.shape[1]
    product = jnp.dot(acts_ref[...], weight_ref[...], preferred_element_type=jnp.float32)
    for block in range(out_ref.shape[1] // width):
        @pl.when(step == block)
        def _():
            out_ref[:, block * width:(block + 1) * width] = product

    if len(rest) == 2:
        @pl.when(step == 0)
        def _():
            out_ref[:, out_ref.shape[1] - rest[0].shape[0]:] = contract_last(acts_ref[...], rest[0][...])


def product(half, tokens, weight, *down):
    rows, depth = tokens.shape
    narrow = weight.shape[1] // 2
    width = 256
    blocks = narrow // width
    out = jax.ShapeDtypeStruct((rows, narrow + sum(each.shape[0] for each in down)), jnp.float32)

    def whole(step, half_ref):
        return 0, 0

    return pl.pallas_call(
        product_kernel,
        out_shape=out,
        grid_spec=pltpu.PrefetchScalarGridSpec(
            num_scalar_prefetch=1,
            grid=(blocks,),
            in_specs=[
                pl.BlockSpec(tokens.shape, whole),
                pl.BlockSpec((depth, width), lambda step, half_ref: (0, half_ref[0] * blocks + step)),
                *[pl.BlockSpec(each.shape, whole) for each in down],
            ],
            out_specs=pl.BlockSpec(out.shape, whole),
        ),
        compiler_params=pltpu.CompilerParams(vmem_limit_bytes=44 << 20),
        cost_estimate=pl.CostEstimate(flops=0, bytes_accessed=0, transcendentals=0),
    )(half, tokens, weight, *down)


def final_kernel(slots_ref, keep_ref, send_ref, arrived_ref, partial_ref, other_ref, own_up_ref, up_ref, out_ref, own, passed):
    steps, rows, narrow = out_ref.shape
    _, rank, both = up_ref.shape
    held = own_up_ref.shape[0] // rank
    block_rows = rows // slots_ref.shape[1]
    for step in range(steps):
        for block in range(slots_ref.shape[1]):
            slot = slots_ref[step, block]
            here = slice(step * rows + block * block_rows, step * rows + (block + 1) * block_rows)
            mine = (send_ref[here, narrow:] + arrived_ref[here, narrow:]).astype(own.dtype)
            column = lax.broadcasted_iota(jnp.int32, mine.shape, 1) // rank
            own[here] = jnp.where(column == slot, mine, jnp.zeros_like(mine))
            given = (partial_ref[here] + other_ref[here]).astype(passed.dtype)
            passed[here] = jnp.where(slot == held, given, jnp.zeros_like(given))
    for step in range(steps):
        here = slice(step * rows, (step + 1) * rows)
        base = keep_ref[here] + arrived_ref[here, :narrow]
        base += jnp.dot(own[here], own_up_ref[...], preferred_element_type=jnp.float32)
        base += jnp.dot(passed[here], up_ref[step, :, both - narrow:], preferred_element_type=jnp.float32)
        out_ref[step] = base.astype(out_ref.dtype)


def finish(slots, keep, send, arrived, partial, other, own_up, handed):
    steps, rank, _ = handed.shape
    held_rank, narrow = own_up.shape
    rows = keep.shape[0]
    vmem = pl.BlockSpec(memory_space=pltpu.VMEM)
    return pl.pallas_call(
        final_kernel,
        out_shape=jax.ShapeDtypeStruct((steps, rows // steps, narrow), jnp.bfloat16),
        in_specs=[pl.BlockSpec(memory_space=pltpu.SMEM)] + [vmem] * 7,
        out_specs=vmem,
        scratch_shapes=[
            pltpu.VMEM((rows, held_rank), jnp.bfloat16),
            pltpu.VMEM((rows, rank), jnp.bfloat16),
        ],
        compiler_params=pltpu.CompilerParams(vmem_limit_bytes=12 << 20),
    )(slots, keep, send, arrived, partial, other, own_up, handed)


def rank_kernel(acts_ref, handed_ref, out_ref):
    steps, rows, wide = acts_ref.shape
    for step in range(steps):
        out_ref[step * rows:(step + 1) * rows] = contract_last(acts_ref[step], handed_ref[step, :, :wide])


def rank_part(acts, handed):
    steps, rows, _ = acts.shape
    vmem = pl.BlockSpec(memory_space=pltpu.VMEM)
    return pl.pallas_call(
        rank_kernel,
        out_shape=jax.ShapeDtypeStruct((steps * rows, handed.shape[1]), jnp.float32),
        in_specs=[vmem, vmem],
        out_specs=vmem,
        compiler_params=pltpu.CompilerParams(vmem_limit_bytes=16 << 20),
    )(acts, handed)


def body(acts, value_weight, adapter_down, adapter_up, block_slots, transfer_offset, transfer_slot):
    groups, servers = lax.axis_size("groups"), lax.axis_size("adapter")
    parts = STRIPES // groups
    steps, rows_dev, wide = acts.shape
    held, rank, _ = adapter_down.shape
    narrow = adapter_up.shape[2]
    side = lax.axis_index("tensor").astype(jnp.int32)

    stripes = cut_stripes(adapter_down, adapter_up, parts)
    banked = {0: stripes[0]}
    for k in [1, 2, 3, 4, 5, 6, 7, *range(STRIPES, servers)]:
        banked[k] = lax.ppermute(stripes[k % parts], "adapter", [(i, i ^ k) for i in range(servers)])
    early = [1, 2]
    transfer_slot, *arrived = lax.optimization_barrier((transfer_slot, *[banked[k] for k in early]))
    banked.update(zip(early, arrived))
    banked = [banked[k] for k in range(servers)]

    asked = transfer_offset * held + transfer_slot[:, 0]
    asked = lax.all_gather(asked, ("groups", "adapter")).reshape(-1)

    picked = pick_stripes(asked, banked, steps)
    given = {0: picked[0]}
    for k in (4, 1, 2, 7, 3, 5, 6):
        pairs = []
        for g in range(groups):
            for i in range(servers):
                other = (g * parts + i % parts) ^ k
                pairs.append((g * servers + i, (other // parts) * servers + (i // parts) * parts + other % parts))
        given[k] = lax.ppermute(picked[k], ("groups", "adapter"), pairs)
    swap = [(0, 1), (1, 0)]
    tokens = acts.reshape(steps * rows_dev, wide)
    early = [4]
    other_side, *waited = lax.optimization_barrier((1 - side, *[given[k] for k in early]))
    given.update(zip(early, waited))
    send = product(other_side[None], tokens, value_weight, adapter_down.reshape(held * rank, wide))
    arrived = lax.ppermute(send, "tensor", swap)
    later = [1, 2]
    side, send, *waited = lax.optimization_barrier((side, send, *[given[k] for k in later]))
    given.update(zip(later, waited))
    keep = product(side[None], tokens, value_weight)
    late = [k for k in range(1, STRIPES) if k not in early + later]
    keep, arrived, *waited = lax.optimization_barrier((keep, arrived, *[given[k] for k in late]))
    given.update(zip(late, waited))

    handed = jnp.concatenate([given[k] for k in range(STRIPES)], axis=1)
    partial = rank_part(acts, handed)
    other = lax.ppermute(partial, "tensor", swap)
    return finish(
        block_slots, keep, send, arrived, partial, other, adapter_up.reshape(held * rank, narrow), handed)


def solution(mesh):
    in_specs = (
        P("groups", "adapter", "tensor"),
        P("tensor", None),
        P("adapter", None, "tensor"),
        P("adapter", None, "tensor"),
        P("groups", "adapter"),
        P("groups"),
        P("groups", "adapter"),
    )
    out_specs = P("groups", "adapter", "tensor")
    return jax.shard_map(body, mesh=mesh, in_specs=in_specs, out_specs=out_specs, check_vma=False)
```

```python
import functools

import jax
import jax.numpy as jnp
from jax import lax
from jax.experimental import pallas as pl
from jax.experimental.pallas import tpu as pltpu
from jax.sharding import PartitionSpec as P

STRIPES = 8


def contract_last(left, right):
    return lax.dot_general(
        left, right, (((left.ndim - 1,), (right.ndim - 1,)), ((), ())), preferred_element_type=jnp.float32
    )


def place():
    parts = STRIPES // lax.axis_size("groups")
    group, server = lax.axis_index("groups"), lax.axis_index("adapter")
    return group, server, lax.rem(server, parts), lax.div(server, parts)


def cut_kernel(down_ref, up_ref, *outs):
    wide = down_ref.shape[-1]
    group, _, part, _ = place()
    for index, out_ref in enumerate(outs):
        stripe = group * len(outs) + jnp.bitwise_xor(part, index)
        out_ref[:, :, :wide] = down_ref[:, stripe]
        out_ref[:, :, wide:] = up_ref[:, stripe]


def cut_stripes(adapter_down, adapter_up, stripe_count):
    held, rank, wide = adapter_down.shape
    narrow = adapter_up.shape[2]
    rows = rank // STRIPES
    out = jax.ShapeDtypeStruct((held, rows, wide + narrow), adapter_down.dtype)
    vmem = pl.BlockSpec(memory_space=pltpu.VMEM)
    return pl.pallas_call(
        cut_kernel,
        out_shape=[out] * stripe_count,
        in_specs=[vmem, vmem],
        out_specs=[vmem] * stripe_count,
        compiler_params=pltpu.CompilerParams(vmem_limit_bytes=8 << 20),
    )(
        adapter_down.reshape(held, STRIPES, rows, wide),
        adapter_up.reshape(held, STRIPES, rows, narrow),
    )


def pick_kernel(server_count, steps, held, asked_ref, *rest):
    servers, outs, bank = rest[:server_count], rest[server_count:-1], rest[-1]
    for index, ref in enumerate(servers):
        bank[index * held:(index + 1) * held] = ref[...]
    parts = STRIPES // lax.axis_size("groups")
    group, server, part, half = place()
    for index, out_ref in enumerate(outs):
        asker_group = jnp.bitwise_xor(group, index // parts)
        asker = half * parts + jnp.bitwise_xor(part, index % parts)
        for step in range(steps):
            table = asker_group * server_count
            offset = lax.div(asked_ref[(table + asker) * steps + step], held)
            source = lax.rem(asker - offset + server_count, server_count)
            slot = lax.rem(asked_ref[(table + source) * steps + step], held)
            out_ref[step] = bank[jnp.bitwise_xor(source, server) * held + slot]


def pick_stripes(asked, servers, steps):
    held, rows, width = servers[0].shape
    out = jax.ShapeDtypeStruct((steps, rows, width), servers[0].dtype)
    bank_bytes = len(servers) * held * rows * width * 2
    out_bytes = STRIPES * steps * rows * width * 2
    vmem = pl.BlockSpec(memory_space=pltpu.VMEM)
    return pl.pallas_call(
        functools.partial(pick_kernel, len(servers), steps, held),
        out_shape=[out] * STRIPES,
        in_specs=[pl.BlockSpec(memory_space=pltpu.SMEM)] + [vmem] * len(servers),
        out_specs=[vmem] * STRIPES,
        scratch_shapes=[pltpu.VMEM((len(servers) * held, rows, width), servers[0].dtype)],
        compiler_params=pltpu.CompilerParams(vmem_limit_bytes=2 * bank_bytes + out_bytes + (4 << 20)),
    )(asked, *servers)


def product_kernel(half_ref, acts_ref, weight_ref, *rest):
    out_ref = rest[-1]
    step = pl.program_id(0)
    width = weight_ref.shape[1]
    product = jnp.dot(acts_ref[...], weight_ref[...], preferred_element_type=jnp.float32)
    for block in range(out_ref.shape[1] // width):
        @pl.when(step == block)
        def _():
            out_ref[:, block * width:(block + 1) * width] = product

    if len(rest) == 2:
        @pl.when(step == 0)
        def _():
            out_ref[:, out_ref.shape[1] - rest[0].shape[0]:] = contract_last(acts_ref[...], rest[0][...])


def product(half, tokens, weight, *down):
    rows, depth = tokens.shape
    narrow = weight.shape[1] // 2
    width = 256
    blocks = narrow // width
    out = jax.ShapeDtypeStruct((rows, narrow + sum(each.shape[0] for each in down)), jnp.float32)

    def whole(step, half_ref):
        return 0, 0

    return pl.pallas_call(
        product_kernel,
        out_shape=out,
        grid_spec=pltpu.PrefetchScalarGridSpec(
            num_scalar_prefetch=1,
            grid=(blocks,),
            in_specs=[
                pl.BlockSpec(tokens.shape, whole),
                pl.BlockSpec((depth, width), lambda step, half_ref: (0, half_ref[0] * blocks + step)),
                *[pl.BlockSpec(each.shape, whole) for each in down],
            ],
            out_specs=pl.BlockSpec(out.shape, whole),
        ),
        compiler_params=pltpu.CompilerParams(vmem_limit_bytes=44 << 20),
        cost_estimate=pl.CostEstimate(flops=0, bytes_accessed=0, transcendentals=0),
    )(half, tokens, weight, *down)


def final_kernel(slots_ref, keep_ref, send_ref, arrived_ref, partial_ref, other_ref, own_up_ref, up_ref, out_ref, own, passed):
    steps, rows, narrow = out_ref.shape
    _, rank, both = up_ref.shape
    held = own_up_ref.shape[0] // rank
    block_rows = rows // slots_ref.shape[1]
    for step in range(steps):
        for block in range(slots_ref.shape[1]):
            slot = slots_ref[step, block]
            here = slice(step * rows + block * block_rows, step * rows + (block + 1) * block_rows)
            mine = (send_ref[here, narrow:] + arrived_ref[here, narrow:]).astype(own.dtype)
            column = lax.broadcasted_iota(jnp.int32, mine.shape, 1) // rank
            own[here] = jnp.where(column == slot, mine, jnp.zeros_like(mine))
            given = (partial_ref[here] + other_ref[here]).astype(passed.dtype)
            passed[here] = jnp.where(slot == held, given, jnp.zeros_like(given))
    for step in range(steps):
        here = slice(step * rows, (step + 1) * rows)
        base = keep_ref[here] + arrived_ref[here, :narrow]
        base += jnp.dot(own[here], own_up_ref[...], preferred_element_type=jnp.float32)
        base += jnp.dot(passed[here], up_ref[step, :, both - narrow:], preferred_element_type=jnp.float32)
        out_ref[step] = base.astype(out_ref.dtype)


def finish(slots, keep, send, arrived, partial, other, own_up, handed):
    steps, rank, _ = handed.shape
    held_rank, narrow = own_up.shape
    rows = keep.shape[0]
    vmem = pl.BlockSpec(memory_space=pltpu.VMEM)
    return pl.pallas_call(
        final_kernel,
        out_shape=jax.ShapeDtypeStruct((steps, rows // steps, narrow), jnp.bfloat16),
        in_specs=[pl.BlockSpec(memory_space=pltpu.SMEM)] + [vmem] * 7,
        out_specs=vmem,
        scratch_shapes=[
            pltpu.VMEM((rows, held_rank), jnp.bfloat16),
            pltpu.VMEM((rows, rank), jnp.bfloat16),
        ],
        compiler_params=pltpu.CompilerParams(vmem_limit_bytes=12 << 20),
    )(slots, keep, send, arrived, partial, other, own_up, handed)


def rank_kernel(acts_ref, handed_ref, out_ref):
    steps, rows, wide = acts_ref.shape
    for step in range(steps):
        out_ref[step * rows:(step + 1) * rows] = contract_last(acts_ref[step], handed_ref[step, :, :wide])


def rank_part(acts, handed):
    steps, rows, _ = acts.shape
    vmem = pl.BlockSpec(memory_space=pltpu.VMEM)
    return pl.pallas_call(
        rank_kernel,
        out_shape=jax.ShapeDtypeStruct((steps * rows, handed.shape[1]), jnp.float32),
        in_specs=[vmem, vmem],
        out_specs=vmem,
        compiler_params=pltpu.CompilerParams(vmem_limit_bytes=16 << 20),
    )(acts, handed)


def body(acts, value_weight, adapter_down, adapter_up, block_slots, transfer_offset, transfer_slot):
    groups, servers = lax.axis_size("groups"), lax.axis_size("adapter")
    parts = STRIPES // groups
    steps, rows_dev, wide = acts.shape
    held, rank, _ = adapter_down.shape
    narrow = adapter_up.shape[2]
    side = lax.axis_index("tensor").astype(jnp.int32)

    stripes = cut_stripes(adapter_down, adapter_up, parts)
    banked = {0: stripes[0]}
    for k in [1, 2, 3, 4, 5, 6, 7, *range(STRIPES, servers)]:
        banked[k] = lax.ppermute(stripes[k % parts], "adapter", [(i, i ^ k) for i in range(servers)])
    early = [5]
    transfer_slot, *arrived = lax.optimization_barrier((transfer_slot, *[banked[k] for k in early]))
    banked.update(zip(early, arrived))
    banked = [banked[k] for k in range(servers)]

    asked = transfer_offset * held + transfer_slot[:, 0]
    asked = lax.all_gather(asked, ("groups", "adapter")).reshape(-1)

    picked = pick_stripes(asked, banked, steps)
    given = {0: picked[0]}
    for k in (4, 1, 2, 7, 3, 5, 6):
        pairs = []
        for g in range(groups):
            for i in range(servers):
                other = (g * parts + i % parts) ^ k
                pairs.append((g * servers + i, (other // parts) * servers + (i // parts) * parts + other % parts))
        given[k] = lax.ppermute(picked[k], ("groups", "adapter"), pairs)
    swap = [(0, 1), (1, 0)]
    tokens = acts.reshape(steps * rows_dev, wide)
    early = [4]
    other_side, *waited = lax.optimization_barrier((1 - side, *[given[k] for k in early]))
    given.update(zip(early, waited))
    send = product(other_side[None], tokens, value_weight, adapter_down.reshape(held * rank, wide))
    arrived = lax.ppermute(send, "tensor", swap)
    later = [1, 2]
    side, send, *waited = lax.optimization_barrier((side, send, *[given[k] for k in later]))
    given.update(zip(later, waited))
    keep = product(side[None], tokens, value_weight)
    late = [k for k in range(1, STRIPES) if k not in early + later]
    keep, arrived, *waited = lax.optimization_barrier((keep, arrived, *[given[k] for k in late]))
    given.update(zip(late, waited))

    handed = jnp.concatenate([given[k] for k in range(STRIPES)], axis=1)
    partial = rank_part(acts, handed)
    other = lax.ppermute(partial, "tensor", swap)
    return finish(
        block_slots, keep, send, arrived, partial, other, adapter_up.reshape(held * rank, narrow), handed)


def solution(mesh):
    in_specs = (
        P("groups", "adapter", "tensor"),
        P("tensor", None),
        P("adapter", None, "tensor"),
        P("adapter", None, "tensor"),
        P("groups", "adapter"),
        P("groups"),
        P("groups", "adapter"),
    )
    out_specs = P("groups", "adapter", "tensor")
    return jax.shard_map(body, mesh=mesh, in_specs=in_specs, out_specs=out_specs, check_vma=False)
```

```python
import functools

import jax
import jax.numpy as jnp
from jax import lax
from jax.experimental import pallas as pl
from jax.experimental.pallas import tpu as pltpu
from jax.sharding import PartitionSpec as P

STRIPES = 8


def contract_last(left, right):
    return lax.dot_general(
        left, right, (((left.ndim - 1,), (right.ndim - 1,)), ((), ())), preferred_element_type=jnp.float32
    )


def place():
    parts = STRIPES // lax.axis_size("groups")
    group, server = lax.axis_index("groups"), lax.axis_index("adapter")
    return group, server, lax.rem(server, parts), lax.div(server, parts)


def cut_kernel(down_ref, up_ref, *outs):
    wide = down_ref.shape[-1]
    group, _, part, _ = place()
    for index, out_ref in enumerate(outs):
        stripe = group * len(outs) + jnp.bitwise_xor(part, index)
        out_ref[:, :, :wide] = down_ref[:, stripe]
        out_ref[:, :, wide:] = up_ref[:, stripe]


def cut_stripes(adapter_down, adapter_up, stripe_count):
    held, rank, wide = adapter_down.shape
    narrow = adapter_up.shape[2]
    rows = rank // STRIPES
    out = jax.ShapeDtypeStruct((held, rows, wide + narrow), adapter_down.dtype)
    vmem = pl.BlockSpec(memory_space=pltpu.VMEM)
    return pl.pallas_call(
        cut_kernel,
        out_shape=[out] * stripe_count,
        in_specs=[vmem, vmem],
        out_specs=[vmem] * stripe_count,
        compiler_params=pltpu.CompilerParams(vmem_limit_bytes=8 << 20),
    )(
        adapter_down.reshape(held, STRIPES, rows, wide),
        adapter_up.reshape(held, STRIPES, rows, narrow),
    )


def pick_kernel(server_count, steps, held, asked_ref, *rest):
    servers, outs, bank = rest[:server_count], rest[server_count:-1], rest[-1]
    for index, ref in enumerate(servers):
        bank[index * held:(index + 1) * held] = ref[...]
    parts = STRIPES // lax.axis_size("groups")
    group, server, part, half = place()
    for index, out_ref in enumerate(outs):
        asker_group = jnp.bitwise_xor(group, index // parts)
        asker = half * parts + jnp.bitwise_xor(part, index % parts)
        for step in range(steps):
            table = asker_group * server_count
            offset = lax.div(asked_ref[(table + asker) * steps + step], held)
            source = lax.rem(asker - offset + server_count, server_count)
            slot = lax.rem(asked_ref[(table + source) * steps + step], held)
            out_ref[step] = bank[jnp.bitwise_xor(source, server) * held + slot]


def pick_stripes(asked, servers, steps):
    held, rows, width = servers[0].shape
    out = jax.ShapeDtypeStruct((steps, rows, width), servers[0].dtype)
    bank_bytes = len(servers) * held * rows * width * 2
    out_bytes = STRIPES * steps * rows * width * 2
    vmem = pl.BlockSpec(memory_space=pltpu.VMEM)
    return pl.pallas_call(
        functools.partial(pick_kernel, len(servers), steps, held),
        out_shape=[out] * STRIPES,
        in_specs=[pl.BlockSpec(memory_space=pltpu.SMEM)] + [vmem] * len(servers),
        out_specs=[vmem] * STRIPES,
        scratch_shapes=[pltpu.VMEM((len(servers) * held, rows, width), servers[0].dtype)],
        compiler_params=pltpu.CompilerParams(vmem_limit_bytes=2 * bank_bytes + out_bytes + (4 << 20)),
    )(asked, *servers)


def product_kernel(half_ref, acts_ref, weight_ref, *rest):
    out_ref = rest[-1]
    step = pl.program_id(0)
    width = weight_ref.shape[1]
    product = jnp.dot(acts_ref[...], weight_ref[...], preferred_element_type=jnp.float32)
    for block in range(out_ref.shape[1] // width):
        @pl.when(step == block)
        def _():
            out_ref[:, block * width:(block + 1) * width] = product

    if len(rest) == 2:
        @pl.when(step == 0)
        def _():
            out_ref[:, out_ref.shape[1] - rest[0].shape[0]:] = contract_last(acts_ref[...], rest[0][...])


def product(half, tokens, weight, *down):
    rows, depth = tokens.shape
    narrow = weight.shape[1] // 2
    width = 256
    blocks = narrow // width
    out = jax.ShapeDtypeStruct((rows, narrow + sum(each.shape[0] for each in down)), jnp.float32)

    def whole(step, half_ref):
        return 0, 0

    return pl.pallas_call(
        product_kernel,
        out_shape=out,
        grid_spec=pltpu.PrefetchScalarGridSpec(
            num_scalar_prefetch=1,
            grid=(blocks,),
            in_specs=[
                pl.BlockSpec(tokens.shape, whole),
                pl.BlockSpec((depth, width), lambda step, half_ref: (0, half_ref[0] * blocks + step)),
                *[pl.BlockSpec(each.shape, whole) for each in down],
            ],
            out_specs=pl.BlockSpec(out.shape, whole),
        ),
        compiler_params=pltpu.CompilerParams(vmem_limit_bytes=44 << 20),
        cost_estimate=pl.CostEstimate(flops=0, bytes_accessed=0, transcendentals=0),
    )(half, tokens, weight, *down)


def base_kernel(rank, slots_ref, keep_ref, send_ref, arrived_ref, up_ref, out_ref, mask_ref, own):
    rows, narrow = out_ref.shape
    held = up_ref.shape[0] // rank
    steps, blocks = slots_ref.shape
    block_rows = rows // steps // blocks
    for step in range(steps):
        for block in range(blocks):
            slot = slots_ref[step, block]
            start = (step * blocks + block) * block_rows
            here = slice(start, start + block_rows)
            mine = (send_ref[here, narrow:] + arrived_ref[here, narrow:]).astype(own.dtype)
            column = lax.broadcasted_iota(jnp.int32, mine.shape, 1) // rank
            own[here] = jnp.where(column == slot, mine, jnp.zeros_like(mine))
            mask_ref[here] = jnp.full((block_rows, rank), (slot == held).astype(jnp.float32))
    low_rank = jnp.dot(own[...], up_ref[...], preferred_element_type=jnp.float32)
    out_ref[...] = keep_ref[...] + arrived_ref[:, :narrow] + low_rank


def add_base(slots, keep, send, arrived, own_up, rank):
    rows, narrow = keep.shape
    vmem = pl.BlockSpec(memory_space=pltpu.VMEM)
    return pl.pallas_call(
        functools.partial(base_kernel, rank),
        out_shape=[
            jax.ShapeDtypeStruct((rows, narrow), jnp.float32),
            jax.ShapeDtypeStruct((rows, rank), jnp.float32),
        ],
        in_specs=[pl.BlockSpec(memory_space=pltpu.SMEM)] + [vmem] * 4,
        out_specs=[vmem] * 2,
        scratch_shapes=[pltpu.VMEM((rows, own_up.shape[0]), jnp.bfloat16)],
        compiler_params=pltpu.CompilerParams(vmem_limit_bytes=12 << 20),
        cost_estimate=pl.CostEstimate(flops=0, bytes_accessed=0, transcendentals=0),
    )(slots, keep, send, arrived, own_up)


def final_kernel(base_ref, mask_ref, partial_ref, other_ref, up_ref, out_ref):
    steps, rows, narrow = out_ref.shape
    for step in range(steps):
        here = slice(step * rows, (step + 1) * rows)
        reduced = ((partial_ref[here] + other_ref[here]) * mask_ref[here]).astype(jnp.bfloat16)
        up = up_ref[step, :, up_ref.shape[2] - narrow:]
        low_rank = jnp.dot(reduced, up, preferred_element_type=jnp.float32)
        out_ref[step] = (base_ref[here] + low_rank).astype(out_ref.dtype)


def finish(base, mask, partial, other, handed):
    steps = handed.shape[0]
    rows, narrow = base.shape
    vmem = pl.BlockSpec(memory_space=pltpu.VMEM)
    return pl.pallas_call(
        final_kernel,
        out_shape=jax.ShapeDtypeStruct((steps, rows // steps, narrow), jnp.bfloat16),
        in_specs=[vmem] * 5,
        out_specs=vmem,
        compiler_params=pltpu.CompilerParams(vmem_limit_bytes=12 << 20),
    )(base, mask, partial, other, handed)


def rank_kernel(acts_ref, handed_ref, out_ref):
    steps, rows, wide = acts_ref.shape
    for step in range(steps):
        out_ref[step * rows:(step + 1) * rows] = contract_last(acts_ref[step], handed_ref[step, :, :wide])


def rank_part(acts, handed):
    steps, rows, _ = acts.shape
    vmem = pl.BlockSpec(memory_space=pltpu.VMEM)
    return pl.pallas_call(
        rank_kernel,
        out_shape=jax.ShapeDtypeStruct((steps * rows, handed.shape[1]), jnp.float32),
        in_specs=[vmem, vmem],
        out_specs=vmem,
        compiler_params=pltpu.CompilerParams(vmem_limit_bytes=16 << 20),
    )(acts, handed)


def body(acts, value_weight, adapter_down, adapter_up, block_slots, transfer_offset, transfer_slot):
    groups, servers = lax.axis_size("groups"), lax.axis_size("adapter")
    parts = STRIPES // groups
    steps, rows_dev, wide = acts.shape
    held, rank, _ = adapter_down.shape
    narrow = adapter_up.shape[2]
    side = lax.axis_index("tensor").astype(jnp.int32)

    stripes = cut_stripes(adapter_down, adapter_up, parts)
    banked = {0: stripes[0]}
    for k in [1, 2, 3, 4, 5, 6, 7, *range(STRIPES, servers)]:
        banked[k] = lax.ppermute(stripes[k % parts], "adapter", [(i, i ^ k) for i in range(servers)])
    early = [5]
    transfer_slot, *arrived = lax.optimization_barrier((transfer_slot, *[banked[k] for k in early]))
    banked.update(zip(early, arrived))
    banked = [banked[k] for k in range(servers)]

    asked = transfer_offset * held + transfer_slot[:, 0]
    asked = lax.all_gather(asked, ("groups", "adapter")).reshape(-1)

    picked = pick_stripes(asked, banked, steps)
    given = {0: picked[0]}
    for k in (4, 1, 2, 7, 3, 5, 6):
        pairs = []
        for g in range(groups):
            for i in range(servers):
                other = (g * parts + i % parts) ^ k
                pairs.append((g * servers + i, (other // parts) * servers + (i // parts) * parts + other % parts))
        given[k] = lax.ppermute(picked[k], ("groups", "adapter"), pairs)
    swap = [(0, 1), (1, 0)]
    tokens = acts.reshape(steps * rows_dev, wide)
    early = [2]
    other_side, *waited = lax.optimization_barrier((1 - side, *[given[k] for k in early]))
    given.update(zip(early, waited))
    send = product(other_side[None], tokens, value_weight, adapter_down.reshape(held * rank, wide))
    arrived = lax.ppermute(send, "tensor", swap)
    later = [1, 4]
    side, send, *waited = lax.optimization_barrier((side, send, *[given[k] for k in later]))
    given.update(zip(later, waited))
    keep = product(side[None], tokens, value_weight)
    late = [k for k in range(1, STRIPES) if k not in early + later]
    base, mask = add_base(block_slots, keep, send, arrived, adapter_up.reshape(held * rank, narrow), rank)
    base, *waited = lax.optimization_barrier((base, *[given[k] for k in late]))
    given.update(zip(late, waited))

    handed = jnp.concatenate([given[k] for k in range(STRIPES)], axis=1)
    partial = rank_part(acts, handed)
    other = lax.ppermute(partial, "tensor", swap)
    return finish(base, mask, partial, other, handed)


def solution(mesh):
    in_specs = (
        P("groups", "adapter", "tensor"),
        P("tensor", None),
        P("adapter", None, "tensor"),
        P("adapter", None, "tensor"),
        P("groups", "adapter"),
        P("groups"),
        P("groups", "adapter"),
    )
    out_specs = P("groups", "adapter", "tensor")
    return jax.shard_map(body, mesh=mesh, in_specs=in_specs, out_specs=out_specs, check_vma=False)
```

```python
import functools

import jax
import jax.numpy as jnp
from jax import lax
from jax.experimental import pallas as pl
from jax.experimental.pallas import tpu as pltpu
from jax.sharding import PartitionSpec as P

STRIPES = 8


def contract_last(left, right):
    return lax.dot_general(
        left, right, (((left.ndim - 1,), (right.ndim - 1,)), ((), ())), preferred_element_type=jnp.float32
    )


def place():
    parts = STRIPES // lax.axis_size("groups")
    group, server = lax.axis_index("groups"), lax.axis_index("adapter")
    return group, server, lax.rem(server, parts), lax.div(server, parts)


def cut_kernel(down_ref, up_ref, *outs):
    wide = down_ref.shape[-1]
    group, _, part, _ = place()
    for index, out_ref in enumerate(outs):
        stripe = group * len(outs) + jnp.bitwise_xor(part, index)
        out_ref[:, :, :wide] = down_ref[:, stripe]
        out_ref[:, :, wide:] = up_ref[:, stripe]


def cut_stripes(adapter_down, adapter_up, stripe_count):
    held, rank, wide = adapter_down.shape
    narrow = adapter_up.shape[2]
    rows = rank // STRIPES
    out = jax.ShapeDtypeStruct((held, rows, wide + narrow), adapter_down.dtype)
    vmem = pl.BlockSpec(memory_space=pltpu.VMEM)
    return pl.pallas_call(
        cut_kernel,
        out_shape=[out] * stripe_count,
        in_specs=[vmem, vmem],
        out_specs=[vmem] * stripe_count,
        compiler_params=pltpu.CompilerParams(vmem_limit_bytes=8 << 20),
    )(
        adapter_down.reshape(held, STRIPES, rows, wide),
        adapter_up.reshape(held, STRIPES, rows, narrow),
    )


def pick_kernel(server_count, steps, held, asked_ref, *rest):
    servers, outs, bank = rest[:server_count], rest[server_count:-1], rest[-1]
    for index, ref in enumerate(servers):
        bank[index * held:(index + 1) * held] = ref[...]
    parts = STRIPES // lax.axis_size("groups")
    group, server, part, half = place()
    for index, out_ref in enumerate(outs):
        asker_group = jnp.bitwise_xor(group, index // parts)
        asker = half * parts + jnp.bitwise_xor(part, index % parts)
        for step in range(steps):
            table = asker_group * server_count
            offset = lax.div(asked_ref[(table + asker) * steps + step], held)
            source = lax.rem(asker - offset + server_count, server_count)
            slot = lax.rem(asked_ref[(table + source) * steps + step], held)
            out_ref[step] = bank[jnp.bitwise_xor(source, server) * held + slot]


def pick_stripes(asked, servers, steps):
    held, rows, width = servers[0].shape
    out = jax.ShapeDtypeStruct((steps, rows, width), servers[0].dtype)
    bank_bytes = len(servers) * held * rows * width * 2
    out_bytes = STRIPES * steps * rows * width * 2
    vmem = pl.BlockSpec(memory_space=pltpu.VMEM)
    return pl.pallas_call(
        functools.partial(pick_kernel, len(servers), steps, held),
        out_shape=[out] * STRIPES,
        in_specs=[pl.BlockSpec(memory_space=pltpu.SMEM)] + [vmem] * len(servers),
        out_specs=[vmem] * STRIPES,
        scratch_shapes=[pltpu.VMEM((len(servers) * held, rows, width), servers[0].dtype)],
        compiler_params=pltpu.CompilerParams(vmem_limit_bytes=2 * bank_bytes + out_bytes + (4 << 20)),
    )(asked, *servers)


def product_kernel(half_ref, acts_ref, weight_ref, *rest):
    out_ref = rest[-1]
    step = pl.program_id(0)
    width = weight_ref.shape[1]
    product = jnp.dot(acts_ref[...], weight_ref[...], preferred_element_type=jnp.float32)
    for block in range(out_ref.shape[1] // width):
        @pl.when(step == block)
        def _():
            out_ref[:, block * width:(block + 1) * width] = product

    if len(rest) == 2:
        @pl.when(step == 0)
        def _():
            out_ref[:, out_ref.shape[1] - rest[0].shape[0]:] = contract_last(acts_ref[...], rest[0][...])


def product(half, tokens, weight, *down):
    rows, depth = tokens.shape
    narrow = weight.shape[1] // 2
    width = 256
    blocks = narrow // width
    out = jax.ShapeDtypeStruct((rows, narrow + sum(each.shape[0] for each in down)), jnp.float32)

    def whole(step, half_ref):
        return 0, 0

    return pl.pallas_call(
        product_kernel,
        out_shape=out,
        grid_spec=pltpu.PrefetchScalarGridSpec(
            num_scalar_prefetch=1,
            grid=(blocks,),
            in_specs=[
                pl.BlockSpec(tokens.shape, whole),
                pl.BlockSpec((depth, width), lambda step, half_ref: (0, half_ref[0] * blocks + step)),
                *[pl.BlockSpec(each.shape, whole) for each in down],
            ],
            out_specs=pl.BlockSpec(out.shape, whole),
        ),
        compiler_params=pltpu.CompilerParams(vmem_limit_bytes=44 << 20),
        cost_estimate=pl.CostEstimate(flops=0, bytes_accessed=0, transcendentals=0),
    )(half, tokens, weight, *down)


def base_kernel(rank, slots_ref, keep_ref, send_ref, arrived_ref, up_ref, out_ref, mask_ref, own):
    rows, narrow = out_ref.shape
    held = up_ref.shape[0] // rank
    steps, blocks = slots_ref.shape
    block_rows = rows // steps // blocks
    for step in range(steps):
        for block in range(blocks):
            slot = slots_ref[step, block]
            start = (step * blocks + block) * block_rows
            here = slice(start, start + block_rows)
            mine = (send_ref[here, narrow:] + arrived_ref[here, narrow:]).astype(own.dtype)
            column = lax.broadcasted_iota(jnp.int32, mine.shape, 1) // rank
            own[here] = jnp.where(column == slot, mine, jnp.zeros_like(mine))
            mask_ref[here] = jnp.full((block_rows, rank), (slot == held).astype(jnp.float32))
    low_rank = jnp.dot(own[...], up_ref[...], preferred_element_type=jnp.float32)
    out_ref[...] = keep_ref[...] + arrived_ref[:, :narrow] + low_rank


def add_base(slots, keep, send, arrived, own_up, rank):
    rows, narrow = keep.shape
    vmem = pl.BlockSpec(memory_space=pltpu.VMEM)
    return pl.pallas_call(
        functools.partial(base_kernel, rank),
        out_shape=[
            jax.ShapeDtypeStruct((rows, narrow), jnp.float32),
            jax.ShapeDtypeStruct((rows, rank), jnp.float32),
        ],
        in_specs=[pl.BlockSpec(memory_space=pltpu.SMEM)] + [vmem] * 4,
        out_specs=[vmem] * 2,
        scratch_shapes=[pltpu.VMEM((rows, own_up.shape[0]), jnp.bfloat16)],
        compiler_params=pltpu.CompilerParams(vmem_limit_bytes=12 << 20),
        cost_estimate=pl.CostEstimate(flops=0, bytes_accessed=0, transcendentals=0),
    )(slots, keep, send, arrived, own_up)


def final_kernel(base_ref, mask_ref, partial_ref, other_ref, up_ref, out_ref):
    steps, rows, narrow = out_ref.shape
    for step in range(steps):
        here = slice(step * rows, (step + 1) * rows)
        reduced = ((partial_ref[here] + other_ref[here]) * mask_ref[here]).astype(jnp.bfloat16)
        up = up_ref[step, :, up_ref.shape[2] - narrow:]
        low_rank = jnp.dot(reduced, up, preferred_element_type=jnp.float32)
        out_ref[step] = (base_ref[here] + low_rank).astype(out_ref.dtype)


def finish(base, mask, partial, other, handed):
    steps = handed.shape[0]
    rows, narrow = base.shape
    vmem = pl.BlockSpec(memory_space=pltpu.VMEM)
    return pl.pallas_call(
        final_kernel,
        out_shape=jax.ShapeDtypeStruct((steps, rows // steps, narrow), jnp.bfloat16),
        in_specs=[vmem] * 5,
        out_specs=vmem,
        compiler_params=pltpu.CompilerParams(vmem_limit_bytes=12 << 20),
    )(base, mask, partial, other, handed)


def rank_kernel(acts_ref, handed_ref, out_ref):
    steps, rows, wide = acts_ref.shape
    for step in range(steps):
        out_ref[step * rows:(step + 1) * rows] = contract_last(acts_ref[step], handed_ref[step, :, :wide])


def rank_part(acts, handed):
    steps, rows, _ = acts.shape
    vmem = pl.BlockSpec(memory_space=pltpu.VMEM)
    return pl.pallas_call(
        rank_kernel,
        out_shape=jax.ShapeDtypeStruct((steps * rows, handed.shape[1]), jnp.float32),
        in_specs=[vmem, vmem],
        out_specs=vmem,
        compiler_params=pltpu.CompilerParams(vmem_limit_bytes=16 << 20),
    )(acts, handed)


def body(acts, value_weight, adapter_down, adapter_up, block_slots, transfer_offset, transfer_slot):
    groups, servers = lax.axis_size("groups"), lax.axis_size("adapter")
    parts = STRIPES // groups
    steps, rows_dev, wide = acts.shape
    held, rank, _ = adapter_down.shape
    narrow = adapter_up.shape[2]
    side = lax.axis_index("tensor").astype(jnp.int32)

    stripes = cut_stripes(adapter_down, adapter_up, parts)
    banked = {0: stripes[0]}
    for k in [1, 2, 3, 4, 5, 6, 7, *range(STRIPES, servers)]:
        banked[k] = lax.ppermute(stripes[k % parts], "adapter", [(i, i ^ k) for i in range(servers)])
    early = [6]
    transfer_slot, *arrived = lax.optimization_barrier((transfer_slot, *[banked[k] for k in early]))
    banked.update(zip(early, arrived))
    banked = [banked[k] for k in range(servers)]

    asked = transfer_offset * held + transfer_slot[:, 0]
    asked = lax.all_gather(asked, ("groups", "adapter")).reshape(-1)

    picked = pick_stripes(asked, banked, steps)
    given = {0: picked[0]}
    for k in (4, 1, 2, 7, 3, 5, 6):
        pairs = []
        for g in range(groups):
            for i in range(servers):
                other = (g * parts + i % parts) ^ k
                pairs.append((g * servers + i, (other // parts) * servers + (i // parts) * parts + other % parts))
        given[k] = lax.ppermute(picked[k], ("groups", "adapter"), pairs)
    swap = [(0, 1), (1, 0)]
    tokens = acts.reshape(steps * rows_dev, wide)
    early = [2]
    other_side, *waited = lax.optimization_barrier((1 - side, *[given[k] for k in early]))
    given.update(zip(early, waited))
    send = product(other_side[None], tokens, value_weight, adapter_down.reshape(held * rank, wide))
    arrived = lax.ppermute(send, "tensor", swap)
    later = [1, 4]
    side, send, *waited = lax.optimization_barrier((side, send, *[given[k] for k in later]))
    given.update(zip(later, waited))
    keep = product(side[None], tokens, value_weight)
    late = [k for k in range(1, STRIPES) if k not in early + later]
    base, mask = add_base(block_slots, keep, send, arrived, adapter_up.reshape(held * rank, narrow), rank)
    base, *waited = lax.optimization_barrier((base, *[given[k] for k in late]))
    given.update(zip(late, waited))

    handed = jnp.concatenate([given[k] for k in range(STRIPES)], axis=1)
    partial = rank_part(acts, handed)
    other = lax.ppermute(partial, "tensor", swap)
    return finish(base, mask, partial, other, handed)


def solution(mesh):
    in_specs = (
        P("groups", "adapter", "tensor"),
        P("tensor", None),
        P("adapter", None, "tensor"),
        P("adapter", None, "tensor"),
        P("groups", "adapter"),
        P("groups"),
        P("groups", "adapter"),
    )
    out_specs = P("groups", "adapter", "tensor")
    return jax.shard_map(body, mesh=mesh, in_specs=in_specs, out_specs=out_specs, check_vma=False)
```

```python
import functools

import jax
import jax.numpy as jnp
from jax import lax
from jax.experimental import pallas as pl
from jax.experimental.pallas import tpu as pltpu
from jax.sharding import PartitionSpec as P

STRIPES = 8


def contract_last(left, right):
    return lax.dot_general(
        left, right, (((left.ndim - 1,), (right.ndim - 1,)), ((), ())), preferred_element_type=jnp.float32
    )


def place():
    parts = STRIPES // lax.axis_size("groups")
    group, server = lax.axis_index("groups"), lax.axis_index("adapter")
    return group, server, lax.rem(server, parts), lax.div(server, parts)


def cut_kernel(down_ref, up_ref, *outs):
    wide = down_ref.shape[-1]
    group, _, part, _ = place()
    for index, out_ref in enumerate(outs):
        stripe = group * len(outs) + jnp.bitwise_xor(part, index)
        out_ref[:, :, :wide] = down_ref[:, stripe]
        out_ref[:, :, wide:] = up_ref[:, stripe]


def cut_stripes(adapter_down, adapter_up, stripe_count):
    held, rank, wide = adapter_down.shape
    narrow = adapter_up.shape[2]
    rows = rank // STRIPES
    out = jax.ShapeDtypeStruct((held, rows, wide + narrow), adapter_down.dtype)
    vmem = pl.BlockSpec(memory_space=pltpu.VMEM)
    return pl.pallas_call(
        cut_kernel,
        out_shape=[out] * stripe_count,
        in_specs=[vmem, vmem],
        out_specs=[vmem] * stripe_count,
        compiler_params=pltpu.CompilerParams(vmem_limit_bytes=8 << 20),
    )(
        adapter_down.reshape(held, STRIPES, rows, wide),
        adapter_up.reshape(held, STRIPES, rows, narrow),
    )


def pick_kernel(server_count, steps, held, asked_ref, *rest):
    servers, outs, bank = rest[:server_count], rest[server_count:-1], rest[-1]
    for index, ref in enumerate(servers):
        bank[index * held:(index + 1) * held] = ref[...]
    parts = STRIPES // lax.axis_size("groups")
    group, server, part, half = place()
    for index, out_ref in enumerate(outs):
        asker_group = jnp.bitwise_xor(group, index // parts)
        asker = half * parts + jnp.bitwise_xor(part, index % parts)
        for step in range(steps):
            table = asker_group * server_count
            offset = lax.div(asked_ref[(table + asker) * steps + step], held)
            source = lax.rem(asker - offset + server_count, server_count)
            slot = lax.rem(asked_ref[(table + source) * steps + step], held)
            out_ref[step] = bank[jnp.bitwise_xor(source, server) * held + slot]


def pick_stripes(asked, servers, steps):
    held, rows, width = servers[0].shape
    out = jax.ShapeDtypeStruct((steps, rows, width), servers[0].dtype)
    bank_bytes = len(servers) * held * rows * width * 2
    out_bytes = STRIPES * steps * rows * width * 2
    vmem = pl.BlockSpec(memory_space=pltpu.VMEM)
    return pl.pallas_call(
        functools.partial(pick_kernel, len(servers), steps, held),
        out_shape=[out] * STRIPES,
        in_specs=[pl.BlockSpec(memory_space=pltpu.SMEM)] + [vmem] * len(servers),
        out_specs=[vmem] * STRIPES,
        scratch_shapes=[pltpu.VMEM((len(servers) * held, rows, width), servers[0].dtype)],
        compiler_params=pltpu.CompilerParams(vmem_limit_bytes=2 * bank_bytes + out_bytes + (4 << 20)),
    )(asked, *servers)


def product_kernel(half_ref, acts_ref, weight_ref, *rest):
    out_ref = rest[-1]
    step = pl.program_id(0)
    width = weight_ref.shape[1]
    product = jnp.dot(acts_ref[...], weight_ref[...], preferred_element_type=jnp.float32)
    for block in range(out_ref.shape[1] // width):
        @pl.when(step == block)
        def _():
            out_ref[:, block * width:(block + 1) * width] = product

    if len(rest) == 2:
        @pl.when(step == 0)
        def _():
            out_ref[:, out_ref.shape[1] - rest[0].shape[0]:] = contract_last(acts_ref[...], rest[0][...])


def product(half, tokens, weight, *down):
    rows, depth = tokens.shape
    narrow = weight.shape[1] // 2
    width = 256
    blocks = narrow // width
    out = jax.ShapeDtypeStruct((rows, narrow + sum(each.shape[0] for each in down)), jnp.float32)

    def whole(step, half_ref):
        return 0, 0

    return pl.pallas_call(
        product_kernel,
        out_shape=out,
        grid_spec=pltpu.PrefetchScalarGridSpec(
            num_scalar_prefetch=1,
            grid=(blocks,),
            in_specs=[
                pl.BlockSpec(tokens.shape, whole),
                pl.BlockSpec((depth, width), lambda step, half_ref: (0, half_ref[0] * blocks + step)),
                *[pl.BlockSpec(each.shape, whole) for each in down],
            ],
            out_specs=pl.BlockSpec(out.shape, whole),
        ),
        compiler_params=pltpu.CompilerParams(vmem_limit_bytes=44 << 20),
        cost_estimate=pl.CostEstimate(flops=0, bytes_accessed=0, transcendentals=0),
    )(half, tokens, weight, *down)


def base_kernel(rank, slots_ref, keep_ref, send_ref, arrived_ref, up_ref, out_ref, mask_ref, own):
    rows, narrow = out_ref.shape
    held = up_ref.shape[0] // rank
    steps, blocks = slots_ref.shape
    block_rows = rows // steps // blocks
    for step in range(steps):
        for block in range(blocks):
            slot = slots_ref[step, block]
            start = (step * blocks + block) * block_rows
            here = slice(start, start + block_rows)
            mine = (send_ref[here, narrow:] + arrived_ref[here, narrow:]).astype(own.dtype)
            column = lax.broadcasted_iota(jnp.int32, mine.shape, 1) // rank
            own[here] = jnp.where(column == slot, mine, jnp.zeros_like(mine))
            mask_ref[here] = jnp.full((block_rows, rank), (slot == held).astype(jnp.float32))
    low_rank = jnp.dot(own[...], up_ref[...], preferred_element_type=jnp.float32)
    out_ref[...] = keep_ref[...] + arrived_ref[:, :narrow] + low_rank


def add_base(slots, keep, send, arrived, own_up, rank):
    rows, narrow = keep.shape
    vmem = pl.BlockSpec(memory_space=pltpu.VMEM)
    return pl.pallas_call(
        functools.partial(base_kernel, rank),
        out_shape=[
            jax.ShapeDtypeStruct((rows, narrow), jnp.float32),
            jax.ShapeDtypeStruct((rows, rank), jnp.float32),
        ],
        in_specs=[pl.BlockSpec(memory_space=pltpu.SMEM)] + [vmem] * 4,
        out_specs=[vmem] * 2,
        scratch_shapes=[pltpu.VMEM((rows, own_up.shape[0]), jnp.bfloat16)],
        compiler_params=pltpu.CompilerParams(vmem_limit_bytes=12 << 20),
        cost_estimate=pl.CostEstimate(flops=0, bytes_accessed=0, transcendentals=0),
    )(slots, keep, send, arrived, own_up)


def final_kernel(base_ref, mask_ref, partial_ref, other_ref, up_ref, out_ref):
    steps, rows, narrow = out_ref.shape
    for step in range(steps):
        here = slice(step * rows, (step + 1) * rows)
        if step % 2 == 0:
            pair = slice(step // 2 * rows, (step // 2 + 1) * rows)
            both = partial_ref[pair] + other_ref[pair]
        rank = mask_ref.shape[1]
        reduced = (both[:, step % 2 * rank:(step % 2 + 1) * rank] * mask_ref[here]).astype(jnp.bfloat16)
        up = up_ref[step, :, up_ref.shape[2] - narrow:]
        low_rank = jnp.dot(reduced, up, preferred_element_type=jnp.float32)
        out_ref[step] = (base_ref[here] + low_rank).astype(out_ref.dtype)


def finish(base, mask, partial, other, handed):
    steps = handed.shape[0]
    rows, narrow = base.shape
    vmem = pl.BlockSpec(memory_space=pltpu.VMEM)
    return pl.pallas_call(
        final_kernel,
        out_shape=jax.ShapeDtypeStruct((steps, rows // steps, narrow), jnp.bfloat16),
        in_specs=[vmem] * 5,
        out_specs=vmem,
        compiler_params=pltpu.CompilerParams(vmem_limit_bytes=12 << 20),
    )(base, mask, partial, other, handed)


def rank_kernel(acts_ref, handed_ref, out_ref):
    steps, rows, wide = acts_ref.shape
    for step in range(steps):
        place, rank = step // 2 * rows, handed_ref.shape[1]
        out_ref[place:place + rows, step % 2 * rank:(step % 2 + 1) * rank] = contract_last(
            acts_ref[step], handed_ref[step, :, :wide])


def rank_part(acts, handed):
    steps, rows, _ = acts.shape
    vmem = pl.BlockSpec(memory_space=pltpu.VMEM)
    return pl.pallas_call(
        rank_kernel,
        out_shape=jax.ShapeDtypeStruct((steps // 2 * rows, 2 * handed.shape[1]), jnp.float32),
        in_specs=[vmem, vmem],
        out_specs=vmem,
        compiler_params=pltpu.CompilerParams(vmem_limit_bytes=16 << 20),
    )(acts, handed)


def body(acts, value_weight, adapter_down, adapter_up, block_slots, transfer_offset, transfer_slot):
    groups, servers = lax.axis_size("groups"), lax.axis_size("adapter")
    parts = STRIPES // groups
    steps, rows_dev, wide = acts.shape
    held, rank, _ = adapter_down.shape
    narrow = adapter_up.shape[2]
    side = lax.axis_index("tensor").astype(jnp.int32)

    stripes = cut_stripes(adapter_down, adapter_up, parts)
    banked = {0: stripes[0]}
    for k in [1, 2, 3, 4, 5, 6, 7, *range(STRIPES, servers)]:
        banked[k] = lax.ppermute(stripes[k % parts], "adapter", [(i, i ^ k) for i in range(servers)])
    early = [6]
    transfer_slot, *arrived = lax.optimization_barrier((transfer_slot, *[banked[k] for k in early]))
    banked.update(zip(early, arrived))
    banked = [banked[k] for k in range(servers)]

    asked = transfer_offset * held + transfer_slot[:, 0]
    asked = lax.all_gather(asked, ("groups", "adapter")).reshape(-1)

    picked = pick_stripes(asked, banked, steps)
    given = {0: picked[0]}
    for k in (7, 3, 4, 1, 2, 6, 5):
        pairs = []
        for g in range(groups):
            for i in range(servers):
                other = (g * parts + i % parts) ^ k
                pairs.append((g * servers + i, (other // parts) * servers + (i // parts) * parts + other % parts))
        given[k] = lax.ppermute(picked[k], ("groups", "adapter"), pairs)
    swap = [(0, 1), (1, 0)]
    tokens = acts.reshape(steps * rows_dev, wide)
    early = [2]
    other_side, *waited = lax.optimization_barrier((1 - side, *[given[k] for k in early]))
    given.update(zip(early, waited))
    send = product(other_side[None], tokens, value_weight, adapter_down.reshape(held * rank, wide))
    arrived = lax.ppermute(send, "tensor", swap)
    later = [1, 4]
    side, send, *waited = lax.optimization_barrier((side, send, *[given[k] for k in later]))
    given.update(zip(later, waited))
    keep = product(side[None], tokens, value_weight)
    late = [k for k in range(1, STRIPES) if k not in early + later]
    base, mask = add_base(block_slots, keep, send, arrived, adapter_up.reshape(held * rank, narrow), rank)
    base, *waited = lax.optimization_barrier((base, *[given[k] for k in late]))
    given.update(zip(late, waited))

    handed = jnp.concatenate([given[k] for k in range(STRIPES)], axis=1)
    partial = rank_part(acts, handed)
    other = lax.ppermute(partial, "tensor", swap)
    return finish(base, mask, partial, other, handed)


def solution(mesh):
    in_specs = (
        P("groups", "adapter", "tensor"),
        P("tensor", None),
        P("adapter", None, "tensor"),
        P("adapter", None, "tensor"),
        P("groups", "adapter"),
        P("groups"),
        P("groups", "adapter"),
    )
    out_specs = P("groups", "adapter", "tensor")
    return jax.shard_map(body, mesh=mesh, in_specs=in_specs, out_specs=out_specs, check_vma=False)
```

```python
import functools

import jax
import jax.numpy as jnp
from jax import lax
from jax.experimental import pallas as pl
from jax.experimental.pallas import tpu as pltpu
from jax.sharding import PartitionSpec as P

STRIPES = 8


def contract_last(left, right):
    return lax.dot_general(
        left, right, (((left.ndim - 1,), (right.ndim - 1,)), ((), ())), preferred_element_type=jnp.float32
    )


def place():
    parts = STRIPES // lax.axis_size("groups")
    group, server = lax.axis_index("groups"), lax.axis_index("adapter")
    return group, server, lax.rem(server, parts), lax.div(server, parts)


def cut_kernel(down_ref, up_ref, *outs):
    wide = down_ref.shape[-1]
    group, _, part, _ = place()
    for index, out_ref in enumerate(outs):
        stripe = group * len(outs) + jnp.bitwise_xor(part, index)
        out_ref[:, :, :wide] = down_ref[:, stripe]
        out_ref[:, :, wide:] = up_ref[:, stripe]


def cut_stripes(adapter_down, adapter_up, stripe_count):
    held, rank, wide = adapter_down.shape
    narrow = adapter_up.shape[2]
    rows = rank // STRIPES
    out = jax.ShapeDtypeStruct((held, rows, wide + narrow), adapter_down.dtype)
    vmem = pl.BlockSpec(memory_space=pltpu.VMEM)
    return pl.pallas_call(
        cut_kernel,
        out_shape=[out] * stripe_count,
        in_specs=[vmem, vmem],
        out_specs=[vmem] * stripe_count,
        compiler_params=pltpu.CompilerParams(vmem_limit_bytes=8 << 20),
    )(
        adapter_down.reshape(held, STRIPES, rows, wide),
        adapter_up.reshape(held, STRIPES, rows, narrow),
    )


def pick_kernel(server_count, steps, held, asked_ref, *rest):
    servers, outs, bank = rest[:server_count], rest[server_count:-1], rest[-1]
    for index, ref in enumerate(servers):
        bank[index * held:(index + 1) * held] = ref[...]
    parts = STRIPES // lax.axis_size("groups")
    group, server, part, half = place()
    for index, out_ref in enumerate(outs):
        asker_group = jnp.bitwise_xor(group, index // parts)
        asker = half * parts + jnp.bitwise_xor(part, index % parts)
        for step in range(steps):
            table = asker_group * server_count
            offset = lax.div(asked_ref[(table + asker) * steps + step], held)
            source = lax.rem(asker - offset + server_count, server_count)
            slot = lax.rem(asked_ref[(table + source) * steps + step], held)
            out_ref[step] = bank[jnp.bitwise_xor(source, server) * held + slot]


def pick_stripes(asked, servers, steps):
    held, rows, width = servers[0].shape
    out = jax.ShapeDtypeStruct((steps, rows, width), servers[0].dtype)
    bank_bytes = len(servers) * held * rows * width * 2
    out_bytes = STRIPES * steps * rows * width * 2
    vmem = pl.BlockSpec(memory_space=pltpu.VMEM)
    return pl.pallas_call(
        functools.partial(pick_kernel, len(servers), steps, held),
        out_shape=[out] * STRIPES,
        in_specs=[pl.BlockSpec(memory_space=pltpu.SMEM)] + [vmem] * len(servers),
        out_specs=[vmem] * STRIPES,
        scratch_shapes=[pltpu.VMEM((len(servers) * held, rows, width), servers[0].dtype)],
        compiler_params=pltpu.CompilerParams(vmem_limit_bytes=2 * bank_bytes + out_bytes + (4 << 20)),
    )(asked, *servers)


def product_kernel(half_ref, acts_ref, weight_ref, *rest):
    out_ref = rest[-1]
    step = pl.program_id(0)
    width = weight_ref.shape[1]
    product = jnp.dot(acts_ref[...], weight_ref[...], preferred_element_type=jnp.float32)
    for block in range(out_ref.shape[1] // width):
        @pl.when(step == block)
        def _():
            out_ref[:, block * width:(block + 1) * width] = product

    if len(rest) == 2:
        @pl.when(step == 0)
        def _():
            out_ref[:, out_ref.shape[1] - rest[0].shape[0]:] = contract_last(acts_ref[...], rest[0][...])


def product(half, tokens, weight, *down):
    rows, depth = tokens.shape
    narrow = weight.shape[1] // 2
    width = 256
    blocks = narrow // width
    out = jax.ShapeDtypeStruct((rows, narrow + sum(each.shape[0] for each in down)), jnp.float32)

    def whole(step, half_ref):
        return 0, 0

    return pl.pallas_call(
        product_kernel,
        out_shape=out,
        grid_spec=pltpu.PrefetchScalarGridSpec(
            num_scalar_prefetch=1,
            grid=(blocks,),
            in_specs=[
                pl.BlockSpec(tokens.shape, whole),
                pl.BlockSpec((depth, width), lambda step, half_ref: (0, half_ref[0] * blocks + step)),
                *[pl.BlockSpec(each.shape, whole) for each in down],
            ],
            out_specs=pl.BlockSpec(out.shape, whole),
        ),
        compiler_params=pltpu.CompilerParams(vmem_limit_bytes=44 << 20),
        cost_estimate=pl.CostEstimate(flops=0, bytes_accessed=0, transcendentals=0),
    )(half, tokens, weight, *down)


def base_kernel(rank, slots_ref, keep_ref, send_ref, arrived_ref, up_ref, out_ref, mask_ref, own):
    rows, narrow = out_ref.shape
    held = up_ref.shape[0] // rank
    steps, blocks = slots_ref.shape
    block_rows = rows // steps // blocks
    for step in range(steps):
        for block in range(blocks):
            slot = slots_ref[step, block]
            start = (step * blocks + block) * block_rows
            here = slice(start, start + block_rows)
            mine = (send_ref[here, narrow:] + arrived_ref[here, narrow:]).astype(own.dtype)
            column = lax.broadcasted_iota(jnp.int32, mine.shape, 1) // rank
            own[here] = jnp.where(column == slot, mine, jnp.zeros_like(mine))
            mask_ref[here] = jnp.full((block_rows, rank), (slot == held).astype(jnp.float32))
    low_rank = jnp.dot(own[...], up_ref[...], preferred_element_type=jnp.float32)
    out_ref[...] = keep_ref[...] + arrived_ref[:, :narrow] + low_rank


def add_base(slots, keep, send, arrived, own_up, rank):
    rows, narrow = keep.shape
    vmem = pl.BlockSpec(memory_space=pltpu.VMEM)
    return pl.pallas_call(
        functools.partial(base_kernel, rank),
        out_shape=[
            jax.ShapeDtypeStruct((rows, narrow), jnp.float32),
            jax.ShapeDtypeStruct((rows, rank), jnp.float32),
        ],
        in_specs=[pl.BlockSpec(memory_space=pltpu.SMEM)] + [vmem] * 4,
        out_specs=[vmem] * 2,
        scratch_shapes=[pltpu.VMEM((rows, own_up.shape[0]), jnp.bfloat16)],
        compiler_params=pltpu.CompilerParams(vmem_limit_bytes=12 << 20),
        cost_estimate=pl.CostEstimate(flops=0, bytes_accessed=0, transcendentals=0),
    )(slots, keep, send, arrived, own_up)


def final_kernel(base_ref, mask_ref, partial_ref, other_ref, up_ref, out_ref):
    steps, rows, narrow = out_ref.shape
    for step in range(steps):
        here = slice(step * rows, (step + 1) * rows)
        if step % 2 == 0:
            pair = slice(step // 2 * rows, (step // 2 + 1) * rows)
            both = partial_ref[pair] + other_ref[pair]
        rank = mask_ref.shape[1]
        reduced = (both[:, step % 2 * rank:(step % 2 + 1) * rank] * mask_ref[here]).astype(jnp.bfloat16)
        up = up_ref[step, :, up_ref.shape[2] - narrow:]
        low_rank = jnp.dot(reduced, up, preferred_element_type=jnp.float32)
        out_ref[step] = (base_ref[here] + low_rank).astype(out_ref.dtype)


def finish(base, mask, partial, other, handed):
    steps = handed.shape[0]
    rows, narrow = base.shape
    vmem = pl.BlockSpec(memory_space=pltpu.VMEM)
    return pl.pallas_call(
        final_kernel,
        out_shape=jax.ShapeDtypeStruct((steps, rows // steps, narrow), jnp.bfloat16),
        in_specs=[vmem] * 5,
        out_specs=vmem,
        compiler_params=pltpu.CompilerParams(vmem_limit_bytes=12 << 20),
    )(base, mask, partial, other, handed)


def rank_kernel(acts_ref, handed_ref, out_ref):
    steps, rows, wide = acts_ref.shape
    for step in range(steps):
        place, rank = step // 2 * rows, handed_ref.shape[1]
        out_ref[place:place + rows, step % 2 * rank:(step % 2 + 1) * rank] = contract_last(
            acts_ref[step], handed_ref[step, :, :wide])


def rank_part(acts, handed):
    steps, rows, _ = acts.shape
    vmem = pl.BlockSpec(memory_space=pltpu.VMEM)
    return pl.pallas_call(
        rank_kernel,
        out_shape=jax.ShapeDtypeStruct((steps // 2 * rows, 2 * handed.shape[1]), jnp.float32),
        in_specs=[vmem, vmem],
        out_specs=vmem,
        compiler_params=pltpu.CompilerParams(vmem_limit_bytes=16 << 20),
    )(acts, handed)


def body(acts, value_weight, adapter_down, adapter_up, block_slots, transfer_offset, transfer_slot):
    groups, servers = lax.axis_size("groups"), lax.axis_size("adapter")
    parts = STRIPES // groups
    steps, rows_dev, wide = acts.shape
    held, rank, _ = adapter_down.shape
    narrow = adapter_up.shape[2]
    side = lax.axis_index("tensor").astype(jnp.int32)

    stripes = cut_stripes(adapter_down, adapter_up, parts)
    banked = {0: stripes[0]}
    for k in [1, 2, 3, 4, 5, 6, 7, *range(STRIPES, servers)]:
        banked[k] = lax.ppermute(stripes[k % parts], "adapter", [(i, i ^ k) for i in range(servers)])
    early = [2, 6]
    transfer_slot, *arrived = lax.optimization_barrier((transfer_slot, *[banked[k] for k in early]))
    banked.update(zip(early, arrived))
    banked = [banked[k] for k in range(servers)]

    asked = transfer_offset * held + transfer_slot[:, 0]
    asked = lax.all_gather(asked, ("groups", "adapter")).reshape(-1)

    picked = pick_stripes(asked, banked, steps)
    given = {0: picked[0]}
    for k in (7, 3, 4, 1, 2, 6, 5):
        pairs = []
        for g in range(groups):
            for i in range(servers):
                other = (g * parts + i % parts) ^ k
                pairs.append((g * servers + i, (other // parts) * servers + (i // parts) * parts + other % parts))
        given[k] = lax.ppermute(picked[k], ("groups", "adapter"), pairs)
    swap = [(0, 1), (1, 0)]
    tokens = acts.reshape(steps * rows_dev, wide)
    early = [2]
    other_side, *waited = lax.optimization_barrier((1 - side, *[given[k] for k in early]))
    given.update(zip(early, waited))
    send = product(other_side[None], tokens, value_weight, adapter_down.reshape(held * rank, wide))
    arrived = lax.ppermute(send, "tensor", swap)
    later = [1, 4]
    side, send, *waited = lax.optimization_barrier((side, send, *[given[k] for k in later]))
    given.update(zip(later, waited))
    keep = product(side[None], tokens, value_weight)
    late = [k for k in range(1, STRIPES) if k not in early + later]
    base, mask = add_base(block_slots, keep, send, arrived, adapter_up.reshape(held * rank, narrow), rank)
    base, *waited = lax.optimization_barrier((base, *[given[k] for k in late]))
    given.update(zip(late, waited))

    handed = jnp.concatenate([given[k] for k in range(STRIPES)], axis=1)
    partial = rank_part(acts, handed)
    other = lax.ppermute(partial, "tensor", swap)
    return finish(base, mask, partial, other, handed)


def solution(mesh):
    in_specs = (
        P("groups", "adapter", "tensor"),
        P("tensor", None),
        P("adapter", None, "tensor"),
        P("adapter", None, "tensor"),
        P("groups", "adapter"),
        P("groups"),
        P("groups", "adapter"),
    )
    out_specs = P("groups", "adapter", "tensor")
    return jax.shard_map(body, mesh=mesh, in_specs=in_specs, out_specs=out_specs, check_vma=False)
```
